512 devices in a mesh: gx: 64 (over z, y_hi, x), gy: 8 (over y_lo, core).
Axes of the slice: x: 4, y: 8 (y_hi: 2, y_lo: 4; y = y_hi * 4 + y_lo), z: 8, core: 2. Of those that a mesh axis runs over, the one named last changes fastest.
Arguments:
- offsets: float32 [3, 64, 64, 512], P(None, 'gx', 'gy'), may hold values from 0 to 1
- masses: float32 [64, 64, 512], P('gx', 'gy'), may hold values from 0.02 to 0.2
- kernel: bfloat16 [36, 2, 36, 64, 4096], P(None, None, None, 'gx', 'gy'), may hold values from -1.2 to 3.2, as said below
Outputs:
- acceleration: float32 [3, 64, 64, 512], P(None, 'gx', 'gy')
The draws below stay inside these ranges and needn't reach their ends.
Inputs may be any that keep to these rules, and one draw needn't show every extreme that they name: `kernel`: G is Hermitian in the wavevector: the entry at -k (each component modulo the grid) is the complex conjugate of the entry at k; all entries at the zero wavevector are zero.
All inputs are finite; a program needn't handle non-finite values.
Results may differ from the reference program's by a relative error of at most 0.0003.
Values sent between devices are 32-bit elements; how exact they have to be, the bound alone decides.
No kernel may reach another device: no remote copies, remote signals or barrier semaphores. Data moves between devices by JAX's collectives and lax.ppermute only.
A program may use at most 128 MiB of HBM per device.

```python
import math
import jax
import jax.numpy as jnp
from jax import lax

NX = 64
NY = 64
NZ = 64
BODIES = 8
MOMENTS = 36


KERNEL_GAIN = 0.5


def mirror_axes(values):
    for axis_index in (1, 2, 3):
        values = jnp.roll(jnp.flip(values, axis_index), 1, axis_index)
    return values


def draw_kernel(key, part):
    full_shape = (2, MOMENTS, NY, NZ, NX)
    channel = jnp.arange(MOMENTS, dtype=jnp.int32)
    anchor = (jnp.arange(NY)[:, None, None] == 0) & (jnp.arange(NZ)[None, :, None] == 0) & (jnp.arange(NX)[None, None, :] == 0)

    def one_row(row_index):
        row_key = jax.random.fold_in(key, row_index)
        noise_key, diagonal_key = jax.random.split(row_key)
        jitter = jnp.clip(0.4 * jax.random.normal(noise_key, full_shape, jnp.float32), -2.4, 2.4)
        diagonal = jnp.exp(jax.random.uniform(diagonal_key, (NY, NZ, NX), jnp.float32, 0.0, math.log(4.0)))
        real_part = jitter[0] + jnp.where((channel == row_index)[:, None, None, None], diagonal[None], 0.0)
        imag_part = jitter[1]
        real_part = 0.5 * (real_part + mirror_axes(real_part))
        imag_part = 0.5 * (imag_part - mirror_axes(imag_part))
        both_parts = jnp.stack([real_part, imag_part]) * KERNEL_GAIN
        both_parts = jnp.where(anchor[None, None], 0.0, both_parts)
        return both_parts.reshape(2, MOMENTS, NY, NZ * NX)
    return lax.map(one_row, jnp.arange(MOMENTS, dtype=jnp.int32)).astype(jnp.bfloat16)


def level_of(stream_key, extent, pieces, least, largest):
    gain = 1.0
    for dim, parts in pieces:
        draws = jax.random.uniform(jax.random.fold_in(jax.random.fold_in(stream_key, 6), dim), (parts,), jnp.float32, least / len(pieces), largest / len(pieces))
        gain = gain * jnp.repeat(jnp.exp(draws), extent[dim] // parts).reshape((-1,) + (1,) * (len(extent) - 1 - dim))
    return gain


def setup_inputs(seed: int = 0) -> dict:
    seeds = jax.random.split(jax.random.key(seed), 4)
    offsets = jnp.clip(1.0 * jax.random.uniform(seeds[0], (3, NX, NY, BODIES * NZ), jnp.float32) ** level_of(seeds[0], (3, NX, NY, BODIES * NZ), ((1, 64), (2, 8)), -0.2, 0.2), 0.0, 1.0)
    masses = jnp.clip(jnp.exp(math.log(0.2) - 2.3025851 * jax.random.uniform(seeds[1], (NX, NY, BODIES * NZ), jnp.float32) ** level_of(seeds[1], (NX, NY, BODIES * NZ), ((0, 64), (1, 8)), -0.2, 0.2)), 0.02, 0.2)
    kernel = draw_kernel(jax.random.fold_in(seeds[3], 71), 0)
    return dict(offsets=offsets, masses=masses, kernel=kernel)


SOFTEN = 0.5

def channel_list():
    listed = []
    for pow_z in range(2):
        for pow_x in range(6 - pow_z):
            for pow_y in range(6 - pow_z - pow_x):
                listed.append((pow_x, pow_y, pow_z))
    return listed

def powers(values, highest):
    result = [jnp.ones_like(values)]
    for degree in range(highest):
        result.append(result[-1] * values)
    return result

def far_accel(local_field, along_x, along_y, along_z):
    accel = [jnp.zeros_like(along_x[1]) for axis_index in range(3)]
    for chan_index, (pow_x, pow_y, pow_z) in enumerate(channel_list()):
        coefficient = local_field[chan_index][:, :, None, :]
        if pow_x > 0:
            accel[0] = accel[0] - coefficient * (pow_x * along_x[pow_x - 1] * along_y[pow_y] * along_z[pow_z])
        if pow_y > 0:
            accel[1] = accel[1] - coefficient * (pow_y * along_x[pow_x] * along_y[pow_y - 1] * along_z[pow_z])
        if pow_z > 0:
            accel[2] = accel[2] - coefficient * (along_x[pow_x] * along_y[pow_y])
    return jnp.stack(accel)

def near_accel(body_pos, mass_cells):
    summed = jnp.zeros_like(body_pos)
    for shift_x in (-1, 0, 1):
        for shift_y in (-1, 0, 1):
            for shift_z in (-1, 0, 1):
                source = jnp.roll(body_pos, (-shift_x, -shift_y, -shift_z), axis=(1, 2, 4))
                source_mass = jnp.roll(mass_cells, (-shift_x, -shift_y, -shift_z), axis=(0, 1, 3))
                offset_vec = jnp.array([shift_x, shift_y, shift_z], jnp.float32).reshape(3, 1, 1, 1, 1)

                def add_slot(slot_index, running):
                    start = slot_index.astype(jnp.int32)
                    other = lax.dynamic_slice_in_dim(source, start, 1, 3)
                    other_mass = lax.dynamic_slice_in_dim(source_mass, start, 1, 2)
                    separation = other + offset_vec - body_pos
                    distance_sq = lax.optimization_barrier(jnp.sum(separation * separation, axis=0)) + SOFTEN * SOFTEN
                    inverse_r = lax.rsqrt(distance_sq)
                    return running + separation * (other_mass * inverse_r * inverse_r * inverse_r)
                summed = lax.fori_loop(0, BODIES, add_slot, summed)
    return summed

def reference(offsets, masses, kernel):
    body_pos = offsets.reshape(3, NX, NY, BODIES, NZ)
    mass_cells = masses.reshape(NX, NY, BODIES, NZ)
    scaled = 2.0 * body_pos - 1.0
    along_x = powers(scaled[0], 5)
    along_y = powers(scaled[1], 5)
    along_z = powers(scaled[2], 1)
    listed = channel_list()
    moments = jnp.stack([lax.optimization_barrier(jnp.sum(mass_cells * (along_x[pow_x] * along_y[pow_y] * along_z[pow_z]), axis=2)) for pow_x, pow_y, pow_z in listed])
    spectrum = jnp.fft.fftn(moments, axes=(1, 2, 3))
    spectrum = jnp.transpose(spectrum, (0, 2, 3, 1)).reshape(len(listed), NY, NZ * NX)
    spec_real = jnp.real(spectrum)
    spec_imag = jnp.imag(spectrum)

    def apply_row(kernel_row):
        gain_real = kernel_row[0].astype(jnp.float32)
        gain_imag = kernel_row[1].astype(jnp.float32)
        out_real = lax.optimization_barrier(jnp.sum(gain_real * spec_real - gain_imag * spec_imag, axis=0))
        out_imag = lax.optimization_barrier(jnp.sum(gain_real * spec_imag + gain_imag * spec_real, axis=0))
        return (out_real, out_imag)
    local_real, local_imag = lax.map(apply_row, kernel)
    local_spec = lax.complex(local_real, local_imag).reshape(len(listed), NY, NZ, NX)
    local_spec = jnp.transpose(local_spec, (0, 3, 1, 2))
    local_field = jnp.real(jnp.fft.ifftn(local_spec, axes=(1, 2, 3)))
    far_part = far_accel(local_field, along_x, along_y, along_z)
    near_part = near_accel(body_pos, mass_cells)
    return (far_part + near_part).reshape(3, NX, NY, BODIES * NZ)
```

```python
import math

import jax
import jax.numpy as jnp
import numpy as np
from jax import lax
from jax.experimental import pallas as pl
from jax.experimental.pallas import tpu as pltpu
from jax.sharding import PartitionSpec as P

SOFTEN = 0.5
N = 64
KEEP = 5
GROUP = 2 * KEEP
MOMENTS = 36
LANES = 384
VMEM = pltpu.VMEM


def channel_list():
    listed = []
    for pow_z in range(2):
        for pow_x in range(6 - pow_z):
            for pow_y in range(6 - pow_z - pow_x):
                listed.append((pow_x, pow_y, pow_z))
    return listed


def split_np(table):
    high = np.asarray(table, np.float32).astype(jnp.bfloat16)
    low = (np.asarray(table, np.float64) - high.astype(np.float64)).astype(jnp.bfloat16)
    return high, low


def angles(rows, columns):
    product = np.outer(np.asarray(rows), np.asarray(columns)) % N
    return product * (2.0 * math.pi / N)


def kept_kz():
    return np.array([8 * block + offset for block in range(8) for offset in range(KEEP)])


def table_z_forward():
    angle = angles(np.arange(N), kept_kz()).reshape(N, 8, 1, KEEP)
    both = np.concatenate([np.cos(angle), -np.sin(angle)], axis=2).reshape(N, 8 * GROUP)
    both = np.pad(both, ((0, 0), (0, 128 - 8 * GROUP)))
    high, low = split_np(both)
    return np.concatenate([high, low, high, np.zeros_like(high)], axis=0)


def table_left():
    angle = angles(np.arange(N), np.arange(N))
    high, low = split_np(np.concatenate([np.cos(angle), np.sin(angle)], axis=0))
    return np.concatenate([high, low, high], axis=1)


def table_x_forward():
    angle = angles(np.arange(N), np.arange(N))
    high, low = split_np(np.concatenate([np.cos(angle), np.sin(angle)], axis=1))
    return np.concatenate([high, low, high, np.zeros_like(high)], axis=0)


def table_x_inverse():
    angle = angles(np.arange(N), np.arange(N))
    high, low = split_np(np.concatenate([np.cos(angle), np.sin(angle)], axis=1))
    return np.concatenate([high, low, high], axis=1)


def table_z_inverse():
    angle = angles(kept_kz(), np.arange(N)).reshape(8, 1, KEEP, N)
    weight = np.where(np.arange(KEEP) % 4 == 0, 1.0, 2.0).reshape(1, 1, KEEP, 1)
    both = np.concatenate([np.cos(angle), -np.sin(angle)], axis=1) * weight / float(N**3)
    both = np.pad(both.reshape(8 * GROUP, N), ((0, 128 - 8 * GROUP), (0, 0)))
    both = np.concatenate([both, both], axis=1)
    high, low = split_np(both)
    return np.concatenate([high, high, low], axis=0)


def split(value):
    high = value.astype(jnp.bfloat16)
    low = (value - high.astype(jnp.float32)).astype(jnp.bfloat16)
    return high, low


def mxu(left, right):
    return jnp.dot(left, right, preferred_element_type=jnp.float32)


def mxu_nt(left, right):
    return lax.dot_general(
        left, right, (((1,), (1,)), ((), ())), preferred_element_type=jnp.float32
    )


def powers(values, highest):
    result = [None, values]
    for _ in range(highest - 1):
        result.append(result[-1] * values)
    return result


def moments_kernel(offsets, masses, table, chunks, packed, moments):
    mass = masses[0]
    for comp in range(3):
        packed[comp] = offsets[comp, 0]
    packed[3] = mass
    along_x = powers(2.0 * offsets[0, 0] - 1.0, 5)
    along_y = powers(2.0 * offsets[1, 0] - 1.0, 5)
    along_z = 2.0 * offsets[2, 0] - 1.0
    channel = 0
    for pow_z in range(2):
        lead_z = mass * along_z if pow_z else mass
        for pow_x in range(6 - pow_z):
            lead = lead_z * along_x[pow_x] if pow_x else lead_z
            for pow_y in range(6 - pow_z - pow_x):
                term = lead * along_y[pow_y] if pow_y else lead
                part = (term[:, 0:128] + term[:, 128:256]) + (term[:, 256:384] + term[:, 384:512])
                moments[8 * channel : 8 * channel + 8, :] = part + pltpu.roll(part, 64, 1)
                channel += 1
    high, low = split(moments[...])
    lines = mxu(jnp.concatenate([high, low], axis=1), table[...])
    chunks[...] = jnp.zeros_like(chunks)
    for channel in range(MOMENTS):
        rows = lines[8 * channel : 8 * channel + 8]
        for block in range(8):
            chunks[block, :, channel * GROUP : (channel + 1) * GROUP] = rows[
                :, block * GROUP : (block + 1) * GROUP
            ]


def line_transform(lines, table, direction):
    high, low = split(lines)
    both = mxu(table, jnp.concatenate([high, high, low], axis=0))
    cos_part, sin_part = both[:N], both[N:]
    lane = lax.broadcasted_iota(jnp.int32, (1, LANES), 1)
    imag_lane = lax.rem(lane, GROUP) >= KEEP
    swapped = jnp.where(
        imag_lane, pltpu.roll(sin_part, KEEP, 1), pltpu.roll(sin_part, LANES - KEEP, 1)
    )
    factor = jnp.where(imag_lane, -1.0, 1.0) * direction
    return cos_part + swapped * factor


def y_forward_kernel(lines, table, out):
    result = line_transform(lines[...], table[...], 1.0)
    for piece in range(3):
        out[pl.ds(piece, N, stride=3), :] = result[:, 128 * piece : 128 * piece + 128]


def y_inverse_kernel(lines, table, out):
    gathered = jnp.concatenate([lines[pl.ds(piece, N, stride=3), :] for piece in range(3)], axis=1)
    out[...] = line_transform(gathered, table[...], -1.0)


def spectrum_kernel(lines, gains, forward, inverse, out, rows, spec, coeff):
    gathered = jnp.concatenate([lines[pl.ds(piece, N, stride=3), :] for piece in range(3)], axis=1)
    turned = jnp.concatenate([gathered, gathered], axis=0).T
    high, low = split(turned)
    rows[...] = mxu(jnp.concatenate([high, low], axis=1), forward[...])
    first_half = lax.broadcasted_iota(jnp.int32, (1, 128), 1) < N
    real_first, imag_first = [], []
    for kz in range(KEEP):
        real_part = rows[pl.ds(kz, MOMENTS, stride=GROUP), :]
        imag_part = rows[pl.ds(KEEP + kz, MOMENTS, stride=GROUP), :]
        both = jnp.where(first_half, real_part, -real_part) + pltpu.roll(imag_part, N, 1)
        real_first.append(both)
        imag_first.append(pltpu.roll(both, N, 1))
    real_first.append(real_first[-1])
    imag_first.append(imag_first[-1])
    for pair in range(3):
        where = slice(128 * pair, 128 * pair + 128)
        spec[0, :, where] = jnp.where(first_half, real_first[2 * pair], imag_first[2 * pair + 1])
        spec[1, :, where] = jnp.where(first_half, imag_first[2 * pair], real_first[2 * pair + 1])

    def add_channel(channel, running):
        real_sum, imag_sum = running
        gain_real = gains[channel, 0].astype(jnp.float32)
        gain_imag = gains[channel, 1].astype(jnp.float32)
        spec_real = spec[0, pl.ds(channel, 1), :]
        spec_imag = spec[1, pl.ds(channel, 1), :]
        real_sum = real_sum + (gain_real * spec_real - gain_imag * spec_imag)
        imag_sum = imag_sum + (gain_real * spec_imag + gain_imag * spec_real)
        return real_sum, imag_sum

    zero = jnp.zeros((MOMENTS, 128 * 3), jnp.float32)
    real_sum, imag_sum = lax.fori_loop(0, MOMENTS, add_channel, (zero, zero))
    coeff[...] = jnp.zeros_like(coeff)
    for pair in range(3):
        where = slice(128 * pair, 128 * pair + 128)
        real_part, imag_part = real_sum[:, where], imag_sum[:, where]
        real_roll, imag_roll = pltpu.roll(real_part, N, 1), pltpu.roll(imag_part, N, 1)
        for half in range(2):
            kz = 2 * pair + half
            if kz >= KEEP:
                continue
            low_real, high_real = (real_part, real_roll) if half == 0 else (real_roll, real_part)
            low_imag, high_imag = (imag_part, imag_roll) if half == 0 else (imag_roll, imag_part)
            coeff[pl.ds(kz, MOMENTS, stride=GROUP), :] = jnp.where(first_half, low_real, -high_imag)
            coeff[pl.ds(KEEP + kz, MOMENTS, stride=GROUP), :] = jnp.where(
                first_half, low_imag, high_real
            )
    high, low = split(coeff[...])
    result = mxu_nt(inverse[...], jnp.concatenate([high, high, low], axis=1))
    for piece in range(3):
        out[pl.ds(piece, N, stride=3), :] = result[:, 128 * piece : 128 * piece + 128]


def final_kernel(chunks, offsets, near, table, out, lines):
    lines[...] = jnp.zeros_like(lines)
    for channel in range(MOMENTS):
        for block in range(8):
            lines[8 * channel : 8 * channel + 8, block * GROUP : (block + 1) * GROUP] = chunks[
                block, :, channel * GROUP : (channel + 1) * GROUP
            ]
    high, low = split(lines[...])
    field = mxu(jnp.concatenate([high, low, high], axis=1), table[...])
    listed = channel_list()
    place = {powers_of: index for index, powers_of in enumerate(listed)}

    def coefficient(pow_x, pow_y, pow_z):
        index = place[(pow_x, pow_y, pow_z)]
        return field[8 * index : 8 * index + 8, :]

    for tile in range(4):
        where = slice(128 * tile, 128 * tile + 128)
        s = 2.0 * offsets[0, 0, :, where] - 1.0
        t = 2.0 * offsets[1, 0, :, where] - 1.0
        w = 2.0 * offsets[2, 0, :, where] - 1.0
        value, slope_s, slope_t = [], [], []
        for pow_z in range(2):
            inner, inner_slope = [], []
            for pow_x in range(6 - pow_z):
                top = 5 - pow_z - pow_x
                total = coefficient(pow_x, top, pow_z)
                slope = None
                for pow_y in range(top - 1, -1, -1):
                    slope = total if slope is None else slope * t + total
                    total = total * t + coefficient(pow_x, pow_y, pow_z)
                inner.append(total)
                inner_slope.append(slope)
            total, slope = inner[-1], None
            total_t = None
            for pow_x in range(len(inner) - 2, -1, -1):
                slope = total if slope is None else slope * s + total
                total = total * s + inner[pow_x]
                total_t = (
                    inner_slope[pow_x] if total_t is None else total_t * s + inner_slope[pow_x]
                )
            value.append(total)
            slope_s.append(slope)
            slope_t.append(total_t)
        out[0, 0, :, where] = near[0, :, where] - (slope_s[0] + w * slope_s[1])
        out[1, 0, :, where] = near[1, :, where] - (slope_t[0] + w * slope_t[1])
        out[2, 0, :, where] = near[2, :, where] - value[1]


def edge_kernel(before, own, after, first_rows, last_rows):
    for plane, ref in enumerate((before, own, after)):
        for comp in range(4):
            first_rows[4 * plane + comp : 4 * plane + comp + 1, :] = ref[comp, 0:1, :]
            last_rows[4 * plane + comp : 4 * plane + comp + 1, :] = ref[comp, 7:8, :]


def near_kernel(before, own, after, above, below, out, extended):
    for plane, ref in enumerate((before, own, after)):
        for comp in range(4):
            index = 4 * plane + comp
            extended[plane, comp, 8:16, :] = ref[comp] + (float(plane - 1) if comp == 0 else 0.0)
            shift = float(plane - 1) if comp == 0 else 0.0
            extended[plane, comp, 7:8, :] = above[index : index + 1, :] + shift
            extended[plane, comp, 16:17, :] = below[index : index + 1, :] + shift
    first_half = lax.broadcasted_iota(jnp.int32, (8, 128), 1) < N
    lane_z = lax.rem(lax.broadcasted_iota(jnp.int32, (8, 128), 1), N)
    targets = [[own[comp, :, 128 * k : 128 * k + 128] for k in range(4)] for comp in range(3)]

    def add_plane(plane, sums):
        sums = list(sums)
        for shift_y in (-1, 0, 1):
            for pair in range(4):
                window = [
                    extended[plane, comp, 8 + shift_y : 16 + shift_y, 128 * pair : 128 * pair + 128]
                    for comp in range(4)
                ]
                window[1] = window[1] + float(shift_y)
                turned = [pltpu.roll(value, N, 1) for value in window]
                for half in range(2):
                    source = [
                        jnp.where(first_half, a, b) if half == 0 else jnp.where(first_half, b, a)
                        for a, b in zip(window, turned)
                    ]
                    for shift_z in (-1, 0, 1):
                        moved = source
                        if shift_z:
                            moved = [pltpu.roll(v, (128 - shift_z) % 128, 1) for v in source]
                            moved[2] = moved[2] + float(shift_z)
                        for k in range(4):
                            sep = [moved[comp] - targets[comp][k] for comp in range(3)]
                            squared = (sep[0] * sep[0] + sep[1] * sep[1]) + (
                                sep[2] * sep[2] + SOFTEN * SOFTEN
                            )
                            inverse = lax.rsqrt(squared)
                            weight = (moved[3] * inverse) * (inverse * inverse)
                            for comp in range(3):
                                sums[3 * k + comp] = sums[3 * k + comp] + sep[comp] * weight
        return tuple(sums)

    zero = jnp.zeros((8, 128), jnp.float32)
    sums = lax.fori_loop(0, 3, add_plane, (zero,) * 12)
    for k in range(4):
        for comp in range(3):
            out[comp, :, 128 * k : 128 * k + 128] = sums[3 * k + comp]


def shape(*dims, dtype=jnp.float32):
    return jax.ShapeDtypeStruct(dims, dtype)


def call(kernel, outs, scratch, cycles):
    block = pl.BlockSpec(memory_space=pltpu.VMEM)
    return pl.pallas_call(
        kernel,
        out_shape=outs,
        in_specs=[block] * (kernel.__code__.co_argcount - len(jax.tree.leaves(outs)) - len(scratch)),
        out_specs=jax.tree.map(lambda _: block, outs),
        scratch_shapes=scratch,
        compiler_params=pltpu.CompilerParams(vmem_limit_bytes=16 << 20),
        cost_estimate=pl.CostEstimate(flops=cycles * 1000, bytes_accessed=cycles, transcendentals=0),
    )


def shift_axis(value, axis, step):
    count = lax.axis_size(axis)
    return lax.ppermute(value, axis, [(i, (i + step) % count) for i in range(count)])


def exchange_rows(value, axis):
    rows = value.reshape(64, 1, LANES)
    rows = lax.all_to_all(rows, axis, split_axis=0, concat_axis=0, tiled=True)
    return rows.reshape(192, 128)


def stages(offsets, masses, kernel):
    gains = jnp.transpose(kernel[:, :, :, 0, :LANES], (2, 1, 0, 3))
    left = jnp.asarray(table_left())
    chunks, packed = call(
        moments_kernel,
        (shape(8, 8, LANES), shape(4, 8, 512)),
        [VMEM((8 * MOMENTS, 128), jnp.float32)],
        2000,
    )(offsets, masses, jnp.asarray(table_z_forward()))
    chunks = lax.all_to_all(chunks, "gy", split_axis=0, concat_axis=0, tiled=True)
    before = shift_axis(packed, "gx", 1)
    after = shift_axis(packed, "gx", -1)
    lines = call(y_forward_kernel, shape(192, 128), [], 1000)(chunks.reshape(N, LANES), left)
    lines = exchange_rows(lines, "gx")
    first_rows, last_rows = call(
        edge_kernel, (shape(12, 512), shape(12, 512)), [], 200
    )(before, packed, after)
    above = shift_axis(last_rows, "gy", 1)
    below = shift_axis(first_rows, "gy", -1)
    lines = call(
        spectrum_kernel,
        shape(192, 128),
        [
            VMEM((LANES, 128), jnp.float32),
            VMEM((2, MOMENTS, LANES), jnp.float32),
            VMEM((LANES, 128), jnp.float32),
        ],
        3000,
    )(lines, gains, jnp.asarray(table_x_forward()), jnp.asarray(table_x_inverse()))
    lines = exchange_rows(lines, "gx")
    near = call(
        near_kernel, shape(3, 8, 512), [VMEM((3, 4, 24, 512), jnp.float32)], 6000
    )(before, packed, after, above, below)
    lines = call(y_inverse_kernel, shape(N, LANES), [], 1000)(lines, left)
    chunks = lax.all_to_all(
        lines.reshape(8, 8, LANES), "gy", split_axis=0, concat_axis=0, tiled=True
    )
    return call(
        final_kernel, shape(3, 1, 8, 512), [VMEM((8 * MOMENTS, 128), jnp.float32)], 2000
    )(chunks, offsets, near, jnp.asarray(table_z_inverse()))


def solution(mesh):
    placed = (P(None, "gx", "gy", None), P("gx", "gy", None), P(None, None, None, "gx", "gy"))
    return jax.shard_map(
        stages, mesh=mesh, in_specs=placed, out_specs=P(None, "gx", "gy", None), check_vma=False
    )
```

```python
import math

import jax
import jax.numpy as jnp
import numpy as np
from jax import lax
from jax.experimental import pallas as pl
from jax.experimental.pallas import tpu as pltpu
from jax.sharding import PartitionSpec as P

SOFTEN = 0.5
N = 64
KEEP = 5
GROUP = 2 * KEEP
MOMENTS = 36
LANES = 384
VMEM = pltpu.VMEM


def channel_list():
    listed = []
    for pow_z in range(2):
        for pow_x in range(6 - pow_z):
            for pow_y in range(6 - pow_z - pow_x):
                listed.append((pow_x, pow_y, pow_z))
    return listed


def split_np(table):
    high = np.asarray(table, np.float32).astype(jnp.bfloat16)
    low = (np.asarray(table, np.float64) - high.astype(np.float64)).astype(jnp.bfloat16)
    return high, low


def angles(rows, columns):
    product = np.outer(np.asarray(rows), np.asarray(columns)) % N
    return product * (2.0 * math.pi / N)


def kept_kz():
    return np.array([8 * block + offset for block in range(8) for offset in range(KEEP)])


def table_z_forward():
    angle = angles(np.arange(N), kept_kz()).reshape(N, 8, 1, KEEP)
    both = np.concatenate([np.cos(angle), -np.sin(angle)], axis=2).reshape(N, 8 * GROUP)
    both = np.pad(both, ((0, 0), (0, 128 - 8 * GROUP)))
    high, low = split_np(both)
    return np.concatenate([high, low, high, np.zeros_like(high)], axis=0)


def table_left():
    angle = angles(np.arange(N), np.arange(N))
    high, low = split_np(np.concatenate([np.cos(angle), np.sin(angle)], axis=0))
    return np.concatenate([high, low, high], axis=1)


def table_x_forward():
    angle = angles(np.arange(N), np.arange(N))
    high, low = split_np(np.concatenate([np.cos(angle), np.sin(angle)], axis=1))
    return np.concatenate([high, low, high, np.zeros_like(high)], axis=0)


def table_x_inverse():
    angle = angles(np.arange(N), np.arange(N))
    high, low = split_np(np.concatenate([np.cos(angle), np.sin(angle)], axis=1))
    return np.concatenate([high, low, high], axis=1)


def table_z_inverse():
    angle = angles(kept_kz(), np.arange(N)).reshape(8, 1, KEEP, N)
    weight = np.where(np.arange(KEEP) % 4 == 0, 1.0, 2.0).reshape(1, 1, KEEP, 1)
    both = np.concatenate([np.cos(angle), -np.sin(angle)], axis=1) * weight / float(N**3)
    both = np.pad(both.reshape(8 * GROUP, N), ((0, 128 - 8 * GROUP), (0, 0)))
    both = np.concatenate([both, both], axis=1)
    high, low = split_np(both)
    return np.concatenate([high, high, low], axis=0)


def split(value):
    high = value.astype(jnp.bfloat16)
    low = (value - high.astype(jnp.float32)).astype(jnp.bfloat16)
    return high, low


def mxu(left, right):
    return jnp.dot(left, right, preferred_element_type=jnp.float32)


def mxu_nt(left, right):
    return lax.dot_general(
        left, right, (((1,), (1,)), ((), ())), preferred_element_type=jnp.float32
    )


def powers(values, highest):
    result = [None, values]
    for _ in range(highest - 1):
        result.append(result[-1] * values)
    return result


EDGE = 256
ROWS = 4 * 10


def edge_places(comp):
    for tile in range(4):
        index = 4 * comp + tile
        lane = LANES + 128 * (index % 2)
        yield tile, index // 2, slice(lane, lane + 128)


def moments_kernel(
    offsets_hbm,
    masses_hbm,
    table_hbm,
    left_hbm,
    chunks,
    packed,
    left,
    offsets,
    masses,
    table,
    moments,
    sems,
):
    pairs = (
        (offsets_hbm, offsets),
        (masses_hbm, masses),
        (table_hbm, table),
        (left_hbm, left),
    )
    copies = [pltpu.make_async_copy(a, b, sems.at[i]) for i, (a, b) in enumerate(pairs)]
    for copy in copies:
        copy.start()
    me = lax.axis_index("gy")
    after, before = lax.rem(me + 1, 8), lax.rem(me + 7, 8)
    chunks[:, :, 256:] = jnp.zeros((8, 8, LANES + EDGE - 256), jnp.float32)
    copies[0].wait()
    copies[1].wait()
    mass = masses[0]
    for comp in range(4):
        value = offsets[comp, 0] if comp < 3 else mass
        for tile, row, lanes in edge_places(comp):
            part = value[:, 128 * tile : 128 * tile + 128]
            packed[tile, pl.ds(comp, 8, stride=4), :] = part
            chunks[after, row : row + 1, lanes] = part[7:8]
            chunks[before, row : row + 1, lanes] = part[0:1]
    along_x = powers(2.0 * offsets[0, 0] - 1.0, 5)
    along_y = powers(2.0 * offsets[1, 0] - 1.0, 5)
    along_z = 2.0 * offsets[2, 0] - 1.0
    channel = 0
    for pow_z in range(2):
        lead_z = mass * along_z if pow_z else mass
        for pow_x in range(6 - pow_z):
            lead = lead_z * along_x[pow_x] if pow_x else lead_z
            for pow_y in range(6 - pow_z - pow_x):
                term = lead * along_y[pow_y] if pow_y else lead
                part = (term[:, 0:128] + term[:, 128:256]) + (term[:, 256:384] + term[:, 384:512])
                moments[8 * channel : 8 * channel + 8, :] = part + pltpu.roll(part, 64, 1)
                channel += 1
    high, low = split(moments[...])
    copies[2].wait()
    lines = mxu(jnp.concatenate([high, low], axis=1), table[...])
    for channel in range(MOMENTS):
        rows = lines[8 * channel : 8 * channel + 8]
        for block in range(8):
            chunks[block, :, channel * GROUP : (channel + 1) * GROUP] = rows[
                :, block * GROUP : (block + 1) * GROUP
            ]
    copies[3].wait()


def line_transform(lines, table, direction):
    high, low = split(lines)
    both = mxu(table, jnp.concatenate([high, high, low], axis=0))
    cos_part, sin_part = both[:N], both[N:]
    lane = lax.broadcasted_iota(jnp.int32, (1, LANES), 1)
    imag_lane = lax.rem(lane, GROUP) >= KEEP
    swapped = jnp.where(
        imag_lane, pltpu.roll(sin_part, KEEP, 1), pltpu.roll(sin_part, LANES - KEEP, 1)
    )
    factor = jnp.where(imag_lane, -1.0, 1.0) * direction
    return cos_part + swapped * factor


def y_forward_kernel(chunks, packed, table, out, extended):
    result = line_transform(chunks[:, :, :LANES].reshape(N, LANES), table[...], 1.0)
    for piece in range(3):
        out[pl.ds(piece, N, stride=3), :] = result[:, 128 * piece : 128 * piece + 128]
    me = lax.axis_index("gy")
    after, before = lax.rem(me + 1, 8), lax.rem(me + 7, 8)
    extended[:, 4 : ROWS - 4, :] = packed[...]
    for comp in range(4):
        last = ROWS - 4 + comp
        for tile, row, lanes in edge_places(comp):
            extended[tile, comp : comp + 1, :] = chunks[before, row : row + 1, lanes]
            extended[tile, last : last + 1, :] = chunks[after, row : row + 1, lanes]


def y_inverse_kernel(lines, table, out):
    gathered = jnp.concatenate([lines[pl.ds(piece, N, stride=3), :] for piece in range(3)], axis=1)
    out[...] = line_transform(gathered, table[...], -1.0)


def spectrum_kernel(lines, gains, forward, inverse, out, rows, spec, coeff):
    gathered = jnp.concatenate([lines[pl.ds(piece, N, stride=3), :] for piece in range(3)], axis=1)
    turned = jnp.concatenate([gathered, gathered], axis=0).T
    high, low = split(turned)
    rows[...] = mxu(jnp.concatenate([high, low], axis=1), forward[...])
    first_half = lax.broadcasted_iota(jnp.int32, (1, 128), 1) < N
    real_first, imag_first = [], []
    for kz in range(KEEP):
        real_part = rows[pl.ds(kz, MOMENTS, stride=GROUP), :]
        imag_part = rows[pl.ds(KEEP + kz, MOMENTS, stride=GROUP), :]
        both = jnp.where(first_half, real_part, -real_part) + pltpu.roll(imag_part, N, 1)
        real_first.append(both)
        imag_first.append(pltpu.roll(both, N, 1))
    real_first.append(real_first[-1])
    imag_first.append(imag_first[-1])
    for pair in range(3):
        where = slice(128 * pair, 128 * pair + 128)
        spec[0, :, where] = jnp.where(first_half, real_first[2 * pair], imag_first[2 * pair + 1])
        spec[1, :, where] = jnp.where(first_half, imag_first[2 * pair], real_first[2 * pair + 1])

    def add_channel(channel, running):
        real_sum, imag_sum = running
        gain_real = gains[channel, 0].astype(jnp.float32)
        gain_imag = gains[channel, 1].astype(jnp.float32)
        spec_real = spec[0, pl.ds(channel, 1), :]
        spec_imag = spec[1, pl.ds(channel, 1), :]
        real_sum = real_sum + (gain_real * spec_real - gain_imag * spec_imag)
        imag_sum = imag_sum + (gain_real * spec_imag + gain_imag * spec_real)
        return real_sum, imag_sum

    zero = jnp.zeros((MOMENTS, 128 * 3), jnp.float32)
    real_sum, imag_sum = lax.fori_loop(0, MOMENTS, add_channel, (zero, zero))
    coeff[...] = jnp.zeros_like(coeff)
    for pair in range(3):
        where = slice(128 * pair, 128 * pair + 128)
        real_part, imag_part = real_sum[:, where], imag_sum[:, where]
        real_roll, imag_roll = pltpu.roll(real_part, N, 1), pltpu.roll(imag_part, N, 1)
        for half in range(2):
            kz = 2 * pair + half
            if kz >= KEEP:
                continue
            low_real, high_real = (real_part, real_roll) if half == 0 else (real_roll, real_part)
            low_imag, high_imag = (imag_part, imag_roll) if half == 0 else (imag_roll, imag_part)
            coeff[pl.ds(kz, MOMENTS, stride=GROUP), :] = jnp.where(first_half, low_real, -high_imag)
            coeff[pl.ds(KEEP + kz, MOMENTS, stride=GROUP), :] = jnp.where(
                first_half, low_imag, high_real
            )
    high, low = split(coeff[...])
    result = mxu_nt(inverse[...], jnp.concatenate([high, high, low], axis=1))
    for piece in range(3):
        out[pl.ds(piece, N, stride=3), :] = result[:, 128 * piece : 128 * piece + 128]


def final_kernel(chunks, offsets, near, table, out, lines):
    lines[...] = jnp.zeros_like(lines)
    for channel in range(MOMENTS):
        for block in range(8):
            lines[8 * channel : 8 * channel + 8, block * GROUP : (block + 1) * GROUP] = chunks[
                block, :, channel * GROUP : (channel + 1) * GROUP
            ]
    high, low = split(lines[...])
    field = mxu(jnp.concatenate([high, low, high], axis=1), table[...])
    listed = channel_list()
    place = {powers_of: index for index, powers_of in enumerate(listed)}

    def coefficient(pow_x, pow_y, pow_z):
        index = place[(pow_x, pow_y, pow_z)]
        return field[8 * index : 8 * index + 8, :]

    for tile in range(4):
        where = slice(128 * tile, 128 * tile + 128)
        s = 2.0 * offsets[0, 0, :, where] - 1.0
        t = 2.0 * offsets[1, 0, :, where] - 1.0
        w = 2.0 * offsets[2, 0, :, where] - 1.0
        value, slope_s, slope_t = [], [], []
        for pow_z in range(2):
            inner, inner_slope = [], []
            for pow_x in range(6 - pow_z):
                top = 5 - pow_z - pow_x
                total = coefficient(pow_x, top, pow_z)
                slope = None
                for pow_y in range(top - 1, -1, -1):
                    slope = total if slope is None else slope * t + total
                    total = total * t + coefficient(pow_x, pow_y, pow_z)
                inner.append(total)
                inner_slope.append(slope)
            total, slope = inner[-1], None
            total_t = None
            for pow_x in range(len(inner) - 2, -1, -1):
                slope = total if slope is None else slope * s + total
                total = total * s + inner[pow_x]
                total_t = (
                    inner_slope[pow_x] if total_t is None else total_t * s + inner_slope[pow_x]
                )
            value.append(total)
            slope_s.append(slope)
            slope_t.append(total_t)
        out[0, 0, :, where] = near[0, :, where] - (slope_s[0] + w * slope_s[1])
        out[1, 0, :, where] = near[1, :, where] - (slope_t[0] + w * slope_t[1])
        out[2, 0, :, where] = near[2, :, where] - value[1]


def near_kernel(before, own, after, out, planes):
    for plane, ref in enumerate((before, own, after)):
        planes[plane] = ref[...]
    first_half = lax.broadcasted_iota(jnp.int32, (8, 128), 1) < N
    targets = [
        [own[k, pl.ds(4 + comp, 8, stride=4), :] for k in range(4)]
        for comp in range(3)
    ]

    def add_plane(plane, sums):
        sums = list(sums)
        for shift_y in (-1, 0, 1):
            for pair in range(4):
                window = [
                    planes[plane, pair, pl.ds(4 + 4 * shift_y + comp, 8, stride=4), :]
                    for comp in range(4)
                ]
                window[0] = window[0] + (plane - 1).astype(jnp.float32)
                window[1] = window[1] + float(shift_y)
                turned = [pltpu.roll(value, N, 1) for value in window]
                for half in range(2):
                    source = [
                        jnp.where(first_half, a, b) if half == 0 else jnp.where(first_half, b, a)
                        for a, b in zip(window, turned)
                    ]
                    for shift_z in (-1, 0, 1):
                        moved = source
                        if shift_z:
                            moved = [pltpu.roll(v, (128 - shift_z) % 128, 1) for v in source]
                            moved[2] = moved[2] + float(shift_z)
                        for k in range(4):
                            sep = [moved[comp] - targets[comp][k] for comp in range(3)]
                            squared = (sep[0] * sep[0] + sep[1] * sep[1]) + (
                                sep[2] * sep[2] + SOFTEN * SOFTEN
                            )
                            inverse = lax.rsqrt(squared)
                            weight = (moved[3] * inverse) * (inverse * inverse)
                            for comp in range(3):
                                sums[3 * k + comp] = sums[3 * k + comp] + sep[comp] * weight
        return tuple(sums)

    zero = jnp.zeros((8, 128), jnp.float32)
    sums = lax.fori_loop(0, 3, add_plane, (zero,) * 12)
    for k in range(4):
        for comp in range(3):
            out[comp, :, 128 * k : 128 * k + 128] = sums[3 * k + comp]


def shape(*dims, dtype=jnp.float32):
    return jax.ShapeDtypeStruct(dims, dtype)


def call(kernel, outs, scratch, cycles, in_specs=None, out_specs=None, aliases={}):
    block = pl.BlockSpec(memory_space=pltpu.VMEM)
    count = kernel.__code__.co_argcount - len(jax.tree.leaves(outs)) - len(scratch)
    return pl.pallas_call(
        kernel,
        out_shape=outs,
        in_specs=in_specs or [block] * count,
        out_specs=out_specs or jax.tree.map(lambda _: block, outs),
        input_output_aliases=aliases,
        scratch_shapes=scratch,
        compiler_params=pltpu.CompilerParams(vmem_limit_bytes=16 << 20),
        cost_estimate=pl.CostEstimate(flops=cycles * 1000, bytes_accessed=cycles, transcendentals=0),
    )


def far_memory(value):
    return pltpu.with_memory_space_constraint(jnp.asarray(value), pltpu.HBM)


def shift_axis(value, axis, step):
    count = lax.axis_size(axis)
    return lax.ppermute(value, axis, [(i, (i + step) % count) for i in range(count)])


def exchange_rows(value, axis):
    rows = value.reshape(64, 1, LANES)
    rows = lax.all_to_all(rows, axis, split_axis=0, concat_axis=0, tiled=True)
    return rows.reshape(192, 128)


def stages(offsets, masses, kernel):
    hbm = pl.BlockSpec(memory_space=pltpu.HBM)
    table_z, table_y = table_z_forward(), table_left()
    gains = kernel[:, :, :, 0, :LANES]
    chunks, packed, left = call(
        moments_kernel,
        (
            shape(8, 8, LANES + EDGE),
            shape(4, 32, 128),
            shape(*table_y.shape, dtype=jnp.bfloat16),
        ),
        [
            VMEM((3, 1, 8, 512), jnp.float32),
            VMEM((1, 8, 512), jnp.float32),
            VMEM(table_z.shape, jnp.bfloat16),
            VMEM((8 * MOMENTS, 128), jnp.float32),
            pltpu.SemaphoreType.DMA((4,)),
        ],
        2000,
        [hbm] * 4,
    )(*(far_memory(value) for value in (offsets, masses, table_z, table_y)))
    chunks, gains = lax.optimization_barrier((chunks, gains))
    gains = jnp.transpose(gains, (2, 1, 0, 3))
    chunks, gains = lax.optimization_barrier((chunks, gains))
    chunks = lax.all_to_all(chunks, "gy", split_axis=0, concat_axis=0, tiled=True)
    lines, extended = call(
        y_forward_kernel, (shape(192, 128), shape(4, ROWS, 128)), [], 1000
    )(chunks, packed, left)
    lines = exchange_rows(lines, "gx")
    before = shift_axis(extended, "gx", 1)
    after = shift_axis(extended, "gx", -1)
    lines = call(
        spectrum_kernel,
        shape(192, 128),
        [
            VMEM((LANES, 128), jnp.float32),
            VMEM((2, MOMENTS, LANES), jnp.float32),
            VMEM((LANES, 128), jnp.float32),
        ],
        3000,
    )(lines, gains, jnp.asarray(table_x_forward()), jnp.asarray(table_x_inverse()))
    lines = exchange_rows(lines, "gx")
    near = call(near_kernel, shape(3, 8, 512), [VMEM((3, 4, ROWS, 128), jnp.float32)], 6000)(
        before, extended, after
    )
    lines = call(y_inverse_kernel, shape(N, LANES), [], 1000)(lines, left)
    chunks = lax.all_to_all(
        lines.reshape(8, 8, LANES), "gy", split_axis=0, concat_axis=0, tiled=True
    )
    return call(
        final_kernel, shape(3, 1, 8, 512), [VMEM((8 * MOMENTS, 128), jnp.float32)], 2000
    )(chunks, offsets, near, jnp.asarray(table_z_inverse()))


def solution(mesh):
    placed = (P(None, "gx", "gy", None), P("gx", "gy", None), P(None, None, None, "gx", "gy"))
    return jax.shard_map(
        stages, mesh=mesh, in_specs=placed, out_specs=P(None, "gx", "gy", None), check_vma=False
    )
```

```python
import math

import jax
import jax.numpy as jnp
import numpy as np
from jax import lax
from jax.experimental import pallas as pl
from jax.experimental.pallas import tpu as pltpu
from jax.sharding import PartitionSpec as P

SOFTEN = 0.5
N = 64
KEEP = 5
GROUP = 2 * KEEP
MOMENTS = 36
LANES = 384
VMEM = pltpu.VMEM


def channel_list():
    listed = []
    for pow_z in range(2):
        for pow_x in range(6 - pow_z):
            for pow_y in range(6 - pow_z - pow_x):
                listed.append((pow_x, pow_y, pow_z))
    return listed


def split_np(table):
    high = np.asarray(table, np.float32).astype(jnp.bfloat16)
    low = (np.asarray(table, np.float64) - high.astype(np.float64)).astype(jnp.bfloat16)
    return high, low


def angles(rows, columns):
    product = np.outer(np.asarray(rows), np.asarray(columns)) % N
    return product * (2.0 * math.pi / N)


def kept_kz():
    return np.array([8 * block + offset for block in range(8) for offset in range(KEEP)])


def table_z_forward():
    angle = angles(np.arange(N), kept_kz()).reshape(N, 8, 1, KEEP)
    both = np.concatenate([np.cos(angle), -np.sin(angle)], axis=2).reshape(N, 8 * GROUP)
    both = np.pad(both, ((0, 0), (0, 128 - 8 * GROUP)))
    high, low = split_np(both)
    return np.concatenate([high, low, high, np.zeros_like(high)], axis=0)


def table_left():
    angle = angles(np.arange(N), np.arange(N))
    high, low = split_np(np.concatenate([np.cos(angle), np.sin(angle)], axis=0))
    return np.concatenate([high, low, high], axis=1)


def table_x_forward():
    angle = angles(np.arange(N), np.arange(N))
    high, low = split_np(np.concatenate([np.cos(angle), np.sin(angle)], axis=1))
    return np.concatenate([high, low, high, np.zeros_like(high)], axis=0)


def table_x_inverse():
    angle = angles(np.arange(N), np.arange(N))
    high, low = split_np(np.concatenate([np.cos(angle), np.sin(angle)], axis=1))
    return np.concatenate([high, low, high], axis=1)


def table_z_inverse():
    angle = angles(kept_kz(), np.arange(N)).reshape(8, 1, KEEP, N)
    weight = np.where(np.arange(KEEP) % 4 == 0, 1.0, 2.0).reshape(1, 1, KEEP, 1)
    both = np.concatenate([np.cos(angle), -np.sin(angle)], axis=1) * weight / float(N**3)
    both = np.pad(both.reshape(8 * GROUP, N), ((0, 128 - 8 * GROUP), (0, 0)))
    both = np.concatenate([both, both], axis=1)
    high, low = split_np(both)
    return np.concatenate([high, high, low], axis=0)


def split(value):
    high = value.astype(jnp.bfloat16)
    low = (value - high.astype(jnp.float32)).astype(jnp.bfloat16)
    return high, low


def mxu(left, right):
    return jnp.dot(left, right, preferred_element_type=jnp.float32)


def mxu_nt(left, right):
    return lax.dot_general(
        left, right, (((1,), (1,)), ((), ())), preferred_element_type=jnp.float32
    )


def powers(values, highest):
    result = [None, values]
    for _ in range(highest - 1):
        result.append(result[-1] * values)
    return result


EDGE = 256
LEAD = 3
ROWS = 48
FIRST_OWN = LEAD + 4
LAST_EDGE = LEAD + 36
PIECE = 5
CHUNK = 8


def edge_places(comp):
    for tile in range(4):
        index = 4 * comp + tile
        lane = LANES + 128 * (index % 2)
        yield tile, index // 2, slice(lane, lane + 128)


def moments_kernel(
    offsets_hbm,
    masses_hbm,
    table_hbm,
    left_hbm,
    chunks,
    packed,
    left,
    offsets,
    masses,
    table,
    moments,
    sems,
):
    pairs = (
        (offsets_hbm, offsets),
        (masses_hbm, masses),
        (table_hbm, table),
        (left_hbm, left),
    )
    copies = [pltpu.make_async_copy(a, b, sems.at[i]) for i, (a, b) in enumerate(pairs)]
    for copy in copies:
        copy.start()
    me = lax.axis_index("gy")
    after, before = lax.rem(me + 1, 8), lax.rem(me + 7, 8)
    chunks[:, :, 256:] = jnp.zeros((8, 8, LANES + EDGE - 256), jnp.float32)
    copies[0].wait()
    copies[1].wait()
    mass = masses[0]
    for comp in range(4):
        value = offsets[comp, 0] if comp < 3 else mass
        for tile, row, lanes in edge_places(comp):
            part = value[:, 128 * tile : 128 * tile + 128]
            packed[tile, pl.ds(comp, 8, stride=4), :] = part
            chunks[after, row : row + 1, lanes] = part[7:8]
            chunks[before, row : row + 1, lanes] = part[0:1]
    along_x = powers(2.0 * offsets[0, 0] - 1.0, 5)
    along_y = powers(2.0 * offsets[1, 0] - 1.0, 5)
    along_z = 2.0 * offsets[2, 0] - 1.0
    channel = 0
    for pow_z in range(2):
        lead_z = mass * along_z if pow_z else mass
        for pow_x in range(6 - pow_z):
            lead = lead_z * along_x[pow_x] if pow_x else lead_z
            for pow_y in range(6 - pow_z - pow_x):
                term = lead * along_y[pow_y] if pow_y else lead
                part = (term[:, 0:128] + term[:, 128:256]) + (term[:, 256:384] + term[:, 384:512])
                moments[8 * channel : 8 * channel + 8, :] = part + pltpu.roll(part, 64, 1)
                channel += 1
    high, low = split(moments[...])
    copies[2].wait()
    lines = mxu(jnp.concatenate([high, low], axis=1), table[...])
    for channel in range(MOMENTS):
        rows = lines[8 * channel : 8 * channel + 8]
        for block in range(8):
            chunks[block, :, channel * GROUP : (channel + 1) * GROUP] = rows[
                :, block * GROUP : (block + 1) * GROUP
            ]
    copies[3].wait()


def line_transform(lines, table, direction):
    high, low = split(lines)
    both = mxu(table, jnp.concatenate([high, high, low], axis=0))
    cos_part, sin_part = both[:N], both[N:]
    lane = lax.broadcasted_iota(jnp.int32, (1, LANES), 1)
    imag_lane = lax.rem(lane, GROUP) >= KEEP
    swapped = jnp.where(
        imag_lane, pltpu.roll(sin_part, KEEP, 1), pltpu.roll(sin_part, LANES - KEEP, 1)
    )
    factor = jnp.where(imag_lane, -1.0, 1.0) * direction
    return cos_part + swapped * factor


def first_half_lanes():
    return lax.broadcasted_iota(jnp.int32, (CHUNK, 128), 1) < N


def pieces():
    for tile in range(4):
        for group in range(7, -1, -1):
            first = 8 * tile + group
            yield tile, PIECE * group, CHUNK * first, CHUNK * (first + 32)


def gather_lines(lines):
    return jnp.concatenate([lines[pl.ds(row, N, stride=CHUNK), :] for row in range(LEAD)], axis=1)


def scatter_lines(out, result):
    for row in range(LEAD):
        out[pl.ds(row, N, stride=CHUNK), :] = result[:, 128 * row : 128 * row + 128]


def y_forward_kernel(chunks, packed, table, out, extended):
    me = lax.axis_index("gy")
    after, before = lax.rem(me + 1, 8), lax.rem(me + 7, 8)
    extended[:, FIRST_OWN:LAST_EDGE, :] = packed[...]
    for comp in range(4):
        top, bottom = LEAD + comp, LAST_EDGE + comp
        for tile, row, lanes in edge_places(comp):
            extended[tile, top : top + 1, :] = chunks[before, row : row + 1, lanes]
            extended[tile, bottom : bottom + 1, :] = chunks[after, row : row + 1, lanes]
    result = line_transform(chunks[:, :, :LANES].reshape(N, LANES), table[...], 1.0)
    half = first_half_lanes()
    for tile, start, low, high in pieces():
        value = extended[tile, start : start + CHUNK, :]
        turned = pltpu.roll(value, N, 1)
        out[low : low + CHUNK, :] = jnp.where(half, value, turned)
        out[high : high + CHUNK, :] = jnp.where(half, turned, value)
    scatter_lines(out, result)


def y_inverse_kernel(lines, table, out):
    out[...] = line_transform(gather_lines(lines), table[...], -1.0)


def spectrum_kernel(lines, gains, forward, inverse, out, rows, spec, coeff):
    half = first_half_lanes()
    for plane in range(N):
        prior, following = CHUNK * ((plane - 1) % N), CHUNK * ((plane + 1) % N)
        out[CHUNK * plane : CHUNK * plane + CHUNK, :] = jnp.where(
            half, lines[prior : prior + CHUNK, :], lines[following : following + CHUNK, :]
        )
    gathered = gather_lines(lines)
    turned = jnp.concatenate([gathered, gathered], axis=0).T
    high, low = split(turned)
    rows[...] = mxu(jnp.concatenate([high, low], axis=1), forward[...])
    first_half = lax.broadcasted_iota(jnp.int32, (1, 128), 1) < N
    real_first, imag_first = [], []
    for kz in range(KEEP):
        real_part = rows[pl.ds(kz, MOMENTS, stride=GROUP), :]
        imag_part = rows[pl.ds(KEEP + kz, MOMENTS, stride=GROUP), :]
        both = jnp.where(first_half, real_part, -real_part) + pltpu.roll(imag_part, N, 1)
        real_first.append(both)
        imag_first.append(pltpu.roll(both, N, 1))
    real_first.append(real_first[-1])
    imag_first.append(imag_first[-1])
    for pair in range(3):
        where = slice(128 * pair, 128 * pair + 128)
        spec[0, :, where] = jnp.where(first_half, real_first[2 * pair], imag_first[2 * pair + 1])
        spec[1, :, where] = jnp.where(first_half, imag_first[2 * pair], real_first[2 * pair + 1])

    def add_channel(channel, running):
        real_sum, imag_sum = running
        gain_real = gains[channel, 0].astype(jnp.float32)
        gain_imag = gains[channel, 1].astype(jnp.float32)
        spec_real = spec[0, pl.ds(channel, 1), :]
        spec_imag = spec[1, pl.ds(channel, 1), :]
        real_sum = real_sum + (gain_real * spec_real - gain_imag * spec_imag)
        imag_sum = imag_sum + (gain_real * spec_imag + gain_imag * spec_real)
        return real_sum, imag_sum

    zero = jnp.zeros((MOMENTS, 128 * 3), jnp.float32)
    real_sum, imag_sum = lax.fori_loop(0, MOMENTS, add_channel, (zero, zero))
    coeff[...] = jnp.zeros_like(coeff)
    for pair in range(3):
        where = slice(128 * pair, 128 * pair + 128)
        real_part, imag_part = real_sum[:, where], imag_sum[:, where]
        real_roll, imag_roll = pltpu.roll(real_part, N, 1), pltpu.roll(imag_part, N, 1)
        for half in range(2):
            kz = 2 * pair + half
            if kz >= KEEP:
                continue
            low_real, high_real = (real_part, real_roll) if half == 0 else (real_roll, real_part)
            low_imag, high_imag = (imag_part, imag_roll) if half == 0 else (imag_roll, imag_part)
            coeff[pl.ds(kz, MOMENTS, stride=GROUP), :] = jnp.where(first_half, low_real, -high_imag)
            coeff[pl.ds(KEEP + kz, MOMENTS, stride=GROUP), :] = jnp.where(
                first_half, low_imag, high_real
            )
    high, low = split(coeff[...])
    scatter_lines(out, mxu_nt(inverse[...], jnp.concatenate([high, high, low], axis=1)))


def final_kernel(chunks, offsets, near, table, out, lines):
    lines[...] = jnp.zeros_like(lines)
    for channel in range(MOMENTS):
        for block in range(8):
            lines[8 * channel : 8 * channel + 8, block * GROUP : (block + 1) * GROUP] = chunks[
                block, :, channel * GROUP : (channel + 1) * GROUP
            ]
    high, low = split(lines[...])
    field = mxu(jnp.concatenate([high, low, high], axis=1), table[...])
    listed = channel_list()
    place = {powers_of: index for index, powers_of in enumerate(listed)}

    def coefficient(pow_x, pow_y, pow_z):
        index = place[(pow_x, pow_y, pow_z)]
        return field[8 * index : 8 * index + 8, :]

    for tile in range(4):
        where = slice(128 * tile, 128 * tile + 128)
        s = 2.0 * offsets[0, 0, :, where] - 1.0
        t = 2.0 * offsets[1, 0, :, where] - 1.0
        w = 2.0 * offsets[2, 0, :, where] - 1.0
        value, slope_s, slope_t = [], [], []
        for pow_z in range(2):
            inner, inner_slope = [], []
            for pow_x in range(6 - pow_z):
                top = 5 - pow_z - pow_x
                total = coefficient(pow_x, top, pow_z)
                slope = None
                for pow_y in range(top - 1, -1, -1):
                    slope = total if slope is None else slope * t + total
                    total = total * t + coefficient(pow_x, pow_y, pow_z)
                inner.append(total)
                inner_slope.append(slope)
            total, slope = inner[-1], None
            total_t = None
            for pow_x in range(len(inner) - 2, -1, -1):
                slope = total if slope is None else slope * s + total
                total = total * s + inner[pow_x]
                total_t = (
                    inner_slope[pow_x] if total_t is None else total_t * s + inner_slope[pow_x]
                )
            value.append(total)
            slope_s.append(slope)
            slope_t.append(total_t)
        out[0, 0, :, where] = near[0, :, where] - (slope_s[0] + w * slope_s[1])
        out[1, 0, :, where] = near[1, :, where] - (slope_t[0] + w * slope_t[1])
        out[2, 0, :, where] = near[2, :, where] - value[1]


def near_kernel(lines, own, out, planes):
    half = first_half_lanes()
    planes[1] = own[...]
    for tile, start, low, high in pieces():
        left, right = lines[low : low + CHUNK, :], lines[high : high + CHUNK, :]
        planes[0, tile, start : start + CHUNK, :] = jnp.where(half, left, pltpu.roll(right, N, 1))
        planes[2, tile, start : start + CHUNK, :] = jnp.where(half, pltpu.roll(left, N, 1), right)
    first_half = lax.broadcasted_iota(jnp.int32, (8, 128), 1) < N
    targets = [
        [own[k, pl.ds(FIRST_OWN + comp, 8, stride=4), :] for k in range(4)]
        for comp in range(3)
    ]

    def add_plane(plane, sums):
        sums = list(sums)
        for shift_y in (-1, 0, 1):
            for pair in range(4):
                window = [
                    planes[plane, pair, pl.ds(FIRST_OWN + 4 * shift_y + comp, 8, stride=4), :]
                    for comp in range(4)
                ]
                window[0] = window[0] + (plane - 1).astype(jnp.float32)
                window[1] = window[1] + float(shift_y)
                turned = [pltpu.roll(value, N, 1) for value in window]
                for half in range(2):
                    source = [
                        jnp.where(first_half, a, b) if half == 0 else jnp.where(first_half, b, a)
                        for a, b in zip(window, turned)
                    ]
                    for shift_z in (-1, 0, 1):
                        moved = source
                        if shift_z:
                            moved = [pltpu.roll(v, (128 - shift_z) % 128, 1) for v in source]
                            moved[2] = moved[2] + float(shift_z)
                        for k in range(4):
                            sep = [moved[comp] - targets[comp][k] for comp in range(3)]
                            squared = (sep[0] * sep[0] + sep[1] * sep[1]) + (
                                sep[2] * sep[2] + SOFTEN * SOFTEN
                            )
                            inverse = lax.rsqrt(squared)
                            weight = (moved[3] * inverse) * (inverse * inverse)
                            for comp in range(3):
                                sums[3 * k + comp] = sums[3 * k + comp] + sep[comp] * weight
        return tuple(sums)

    zero = jnp.zeros((8, 128), jnp.float32)
    sums = lax.fori_loop(0, 3, add_plane, (zero,) * 12)
    for k in range(4):
        for comp in range(3):
            out[comp, :, 128 * k : 128 * k + 128] = sums[3 * k + comp]


def shape(*dims, dtype=jnp.float32):
    return jax.ShapeDtypeStruct(dims, dtype)


def call(kernel, outs, scratch, cycles, in_specs=None, out_specs=None, aliases={}):
    block = pl.BlockSpec(memory_space=pltpu.VMEM)
    count = kernel.__code__.co_argcount - len(jax.tree.leaves(outs)) - len(scratch)
    return pl.pallas_call(
        kernel,
        out_shape=outs,
        in_specs=in_specs or [block] * count,
        out_specs=out_specs or jax.tree.map(lambda _: block, outs),
        input_output_aliases=aliases,
        scratch_shapes=scratch,
        compiler_params=pltpu.CompilerParams(vmem_limit_bytes=16 << 20),
        cost_estimate=pl.CostEstimate(flops=cycles * 1000, bytes_accessed=cycles, transcendentals=0),
    )


def far_memory(value):
    return pltpu.with_memory_space_constraint(jnp.asarray(value), pltpu.HBM)


def exchange_rows(value, axis):
    rows = value.reshape(N, CHUNK, 128)
    rows = lax.all_to_all(rows, axis, split_axis=0, concat_axis=0, tiled=True)
    return rows.reshape(N * CHUNK, 128)


def stages(offsets, masses, kernel):
    hbm = pl.BlockSpec(memory_space=pltpu.HBM)
    table_z, table_y = table_z_forward(), table_left()
    gains = kernel[:, :, :, 0, :LANES]
    chunks, packed, left = call(
        moments_kernel,
        (
            shape(8, 8, LANES + EDGE),
            shape(4, 32, 128),
            shape(*table_y.shape, dtype=jnp.bfloat16),
        ),
        [
            VMEM((3, 1, 8, 512), jnp.float32),
            VMEM((1, 8, 512), jnp.float32),
            VMEM(table_z.shape, jnp.bfloat16),
            VMEM((8 * MOMENTS, 128), jnp.float32),
            pltpu.SemaphoreType.DMA((4,)),
        ],
        2000,
        [hbm] * 4,
    )(*(far_memory(value) for value in (offsets, masses, table_z, table_y)))
    chunks, gains = lax.optimization_barrier((chunks, gains))
    gains = jnp.transpose(gains, (2, 1, 0, 3))
    chunks, gains = lax.optimization_barrier((chunks, gains))
    chunks = lax.all_to_all(chunks, "gy", split_axis=0, concat_axis=0, tiled=True)
    lines, extended = call(
        y_forward_kernel, (shape(N * CHUNK, 128), shape(4, ROWS, 128)), [], 1000
    )(chunks, packed, left)
    lines = exchange_rows(lines, "gx")
    lines = call(
        spectrum_kernel,
        shape(N * CHUNK, 128),
        [
            VMEM((LANES, 128), jnp.float32),
            VMEM((2, MOMENTS, LANES), jnp.float32),
            VMEM((LANES, 128), jnp.float32),
        ],
        3000,
    )(lines, gains, jnp.asarray(table_x_forward()), jnp.asarray(table_x_inverse()))
    lines = exchange_rows(lines, "gx")
    near = call(near_kernel, shape(3, 8, 512), [VMEM((3, 4, ROWS, 128), jnp.float32)], 6000)(
        lines, extended
    )
    lines = call(y_inverse_kernel, shape(N, LANES), [], 1000)(lines, left)
    chunks = lax.all_to_all(
        lines.reshape(8, 8, LANES), "gy", split_axis=0, concat_axis=0, tiled=True
    )
    return call(
        final_kernel, shape(3, 1, 8, 512), [VMEM((8 * MOMENTS, 128), jnp.float32)], 2000
    )(chunks, offsets, near, jnp.asarray(table_z_inverse()))


def solution(mesh):
    placed = (P(None, "gx", "gy", None), P("gx", "gy", None), P(None, None, None, "gx", "gy"))
    return jax.shard_map(
        stages, mesh=mesh, in_specs=placed, out_specs=P(None, "gx", "gy", None), check_vma=False
    )
```

```python
import math

import jax
import jax.numpy as jnp
import numpy as np
from jax import lax
from jax.experimental import pallas as pl
from jax.experimental.pallas import tpu as pltpu
from jax.sharding import PartitionSpec as P

SOFTEN = 0.5
N = 64
KEEP = 5
GROUP = 2 * KEEP
MOMENTS = 36
LANES = 384
VMEM = pltpu.VMEM


def channel_list():
    listed = []
    for pow_z in range(2):
        for pow_x in range(6 - pow_z):
            for pow_y in range(6 - pow_z - pow_x):
                listed.append((pow_x, pow_y, pow_z))
    return listed


def split_np(table):
    high = np.asarray(table, np.float32).astype(jnp.bfloat16)
    low = (np.asarray(table, np.float64) - high.astype(np.float64)).astype(jnp.bfloat16)
    return high, low


def angles(rows, columns):
    product = np.outer(np.asarray(rows), np.asarray(columns)) % N
    return product * (2.0 * math.pi / N)


def kept_kz():
    return np.array([8 * block + offset for block in range(8) for offset in range(KEEP)])


def table_z_forward():
    angle = angles(np.arange(N), kept_kz()).reshape(N, 8, 1, KEEP)
    both = np.concatenate([np.cos(angle), -np.sin(angle)], axis=2).reshape(N, 8 * GROUP)
    both = np.pad(both, ((0, 0), (0, 128 - 8 * GROUP)))
    high, low = split_np(both)
    return np.concatenate([high, low, high, np.zeros_like(high)], axis=0)


def table_left():
    angle = angles(np.arange(N), np.arange(N))
    high, low = split_np(np.concatenate([np.cos(angle), np.sin(angle)], axis=0))
    return np.concatenate([high, low, high], axis=1)


def table_x_forward():
    angle = angles(np.arange(N), np.arange(N))
    high, low = split_np(np.concatenate([np.cos(angle), np.sin(angle)], axis=1))
    return np.concatenate([high, low, high, np.zeros_like(high)], axis=0)


def table_x_inverse():
    angle = angles(np.arange(N), np.arange(N))
    high, low = split_np(np.concatenate([np.cos(angle), np.sin(angle)], axis=1))
    return np.concatenate([high, low, high], axis=1)


def table_z_inverse():
    angle = angles(kept_kz(), np.arange(N)).reshape(8, 1, KEEP, N)
    weight = np.where(np.arange(KEEP) % 4 == 0, 1.0, 2.0).reshape(1, 1, KEEP, 1)
    both = np.concatenate([np.cos(angle), -np.sin(angle)], axis=1) * weight / float(N**3)
    both = np.pad(both.reshape(8 * GROUP, N), ((0, 128 - 8 * GROUP), (0, 0)))
    both = np.concatenate([both, both], axis=1)
    high, low = split_np(both)
    return np.concatenate([high, high, low], axis=0)


def split(value):
    high = value.astype(jnp.bfloat16)
    low = (value - high.astype(jnp.float32)).astype(jnp.bfloat16)
    return high, low


def mxu(left, right):
    return jnp.dot(left, right, preferred_element_type=jnp.float32)


def mxu_nt(left, right):
    return lax.dot_general(
        left, right, (((1,), (1,)), ((), ())), preferred_element_type=jnp.float32
    )


def powers(values, highest):
    result = [None, values]
    for _ in range(highest - 1):
        result.append(result[-1] * values)
    return result


EDGE = 256
LEAD = 3
TILE_ROWS = 40
PIECES = 54
FLAT = 168
FORWARD, INVERSE = 6, 9


def edge_places(comp):
    for tile in range(4):
        index = 4 * comp + tile
        lane = LANES + 128 * (index % 2)
        yield tile, index // 2, slice(lane, lane + 128)


def moments_kernel(
    offsets_hbm,
    masses_hbm,
    table_hbm,
    left_hbm,
    gains_hbm,
    chunks,
    packed,
    left,
    gains,
    offsets,
    masses,
    table,
    moments,
    sems,
):
    pairs = (
        (offsets_hbm, offsets),
        (masses_hbm, masses),
        (table_hbm, table),
        (left_hbm, left),
    )
    pairs += tuple(
        (gains_hbm.at[row, :, :, pl.ds(0, LANES)], gains.at[:, pl.ds(2 * row, 2), :])
        for row in range(MOMENTS)
    )
    copies = [pltpu.make_async_copy(a, b, sems.at[i]) for i, (a, b) in enumerate(pairs)]
    for copy in copies:
        copy.start()
    me = lax.axis_index("gy")
    after, before = lax.rem(me + 1, 8), lax.rem(me + 7, 8)
    chunks[:, :, 256:] = jnp.zeros((8, 8, LANES + EDGE - 256), jnp.float32)
    copies[0].wait()
    copies[1].wait()
    mass = masses[0]
    for comp in range(4):
        value = offsets[comp, 0] if comp < 3 else mass
        for tile, row, lanes in edge_places(comp):
            part = value[:, 128 * tile : 128 * tile + 128]
            packed[tile, pl.ds(comp, 8, stride=4), :] = part
            chunks[after, row : row + 1, lanes] = part[7:8]
            chunks[before, row : row + 1, lanes] = part[0:1]
    along_x = powers(2.0 * offsets[0, 0] - 1.0, 5)
    along_y = powers(2.0 * offsets[1, 0] - 1.0, 5)
    along_z = 2.0 * offsets[2, 0] - 1.0
    channel = 0
    for pow_z in range(2):
        lead_z = mass * along_z if pow_z else mass
        for pow_x in range(6 - pow_z):
            lead = lead_z * along_x[pow_x] if pow_x else lead_z
            for pow_y in range(6 - pow_z - pow_x):
                term = lead * along_y[pow_y] if pow_y else lead
                part = (term[:, 0:128] + term[:, 128:256]) + (term[:, 256:384] + term[:, 384:512])
                moments[8 * channel : 8 * channel + 8, :] = part + pltpu.roll(part, 64, 1)
                channel += 1
    high, low = split(moments[...])
    copies[2].wait()
    lines = mxu(jnp.concatenate([high, low], axis=1), table[...])
    for channel in range(MOMENTS):
        rows = lines[8 * channel : 8 * channel + 8]
        for block in range(8):
            chunks[block, :, channel * GROUP : (channel + 1) * GROUP] = rows[
                :, block * GROUP : (block + 1) * GROUP
            ]
    for copy in copies[3:]:
        copy.wait()


def line_transform(lines, table, direction):
    high, low = split(lines)
    both = mxu(table, jnp.concatenate([high, high, low], axis=0))
    cos_part, sin_part = both[:N], both[N:]
    lane = lax.broadcasted_iota(jnp.int32, (1, LANES), 1)
    imag_lane = lax.rem(lane, GROUP) >= KEEP
    swapped = jnp.where(
        imag_lane, pltpu.roll(sin_part, KEEP, 1), pltpu.roll(sin_part, LANES - KEEP, 1)
    )
    factor = jnp.where(imag_lane, -1.0, 1.0) * direction
    return cos_part + swapped * factor


def gather_lines(lines, chunk):
    return jnp.concatenate([lines[pl.ds(row, N, stride=chunk), :] for row in range(LEAD)], axis=1)


def scatter_lines(out, result, chunk):
    for row in range(LEAD):
        out[pl.ds(row, N, stride=chunk), :] = result[:, 128 * row : 128 * row + 128]


def y_forward_kernel(chunks, packed, table, out, extended):
    me = lax.axis_index("gy")
    after, before = lax.rem(me + 1, 8), lax.rem(me + 7, 8)
    extended[4 * TILE_ROWS :, :] = jnp.zeros((FLAT - 4 * TILE_ROWS, 128), jnp.float32)
    out[...] = jnp.zeros_like(out)
    for tile in range(4):
        first = TILE_ROWS * tile
        extended[first + 4 : first + 36, :] = packed[tile]
    for comp in range(4):
        for tile, row, lanes in edge_places(comp):
            top = TILE_ROWS * tile + comp
            extended[top : top + 1, :] = chunks[before, row : row + 1, lanes]
            extended[top + 36 : top + 37, :] = chunks[after, row : row + 1, lanes]
    result = line_transform(chunks[:, :, :LANES].reshape(N, LANES), table[...], 1.0)
    scatter_lines(out, result, FORWARD)
    for row in range(3):
        out[pl.ds(LEAD + row, PIECES, stride=FORWARD), :] = extended[pl.ds(row, PIECES, stride=3), :]


def y_inverse_kernel(lines, table, out):
    out[...] = line_transform(gather_lines(lines, INVERSE), table[...], -1.0)


def spectrum_kernel(lines, gains, forward, inverse, out, rows, spec, coeff, sums):
    for row in range(LEAD, 2 * LEAD):
        last, other = N - 1, row + LEAD
        out[pl.ds(INVERSE + row, last, stride=INVERSE), :] = lines[
            pl.ds(row, last, stride=FORWARD), :
        ]
        out[row : row + 1, :] = lines[FORWARD * last + row : FORWARD * last + row + 1, :]
        out[pl.ds(other, last, stride=INVERSE), :] = lines[
            pl.ds(FORWARD + row, last, stride=FORWARD), :
        ]
        out[INVERSE * last + other : INVERSE * last + other + 1, :] = lines[row : row + 1, :]
    gathered = gather_lines(lines, FORWARD)
    turned = jnp.concatenate([gathered, gathered], axis=0).T
    high, low = split(turned)
    rows[...] = mxu(jnp.concatenate([high, low], axis=1), forward[...])
    first_half = lax.broadcasted_iota(jnp.int32, (1, 128), 1) < N
    real_first, imag_first = [], []
    for kz in range(KEEP):
        real_part = rows[pl.ds(kz, MOMENTS, stride=GROUP), :]
        imag_part = rows[pl.ds(KEEP + kz, MOMENTS, stride=GROUP), :]
        both = jnp.where(first_half, real_part, -real_part) + pltpu.roll(imag_part, N, 1)
        real_first.append(both)
        imag_first.append(pltpu.roll(both, N, 1))
    real_first.append(real_first[-1])
    imag_first.append(imag_first[-1])
    for pair in range(3):
        spec[0, pair] = jnp.where(first_half, real_first[2 * pair], imag_first[2 * pair + 1])
        spec[1, pair] = jnp.where(first_half, imag_first[2 * pair], real_first[2 * pair + 1])

    coeff[...] = jnp.zeros_like(coeff)
    for pair in range(3):
        where = slice(128 * pair, 128 * pair + 128)

        def add_channel(channel, running):
            by_real, by_imag = running
            gain = gains[channel, :, where].astype(jnp.float32)
            by_real = by_real + gain * spec[0, pair, pl.ds(channel, 1), :]
            by_imag = by_imag + gain * spec[1, pair, pl.ds(channel, 1), :]
            return by_real, by_imag

        zero = jnp.zeros((2 * MOMENTS, 128), jnp.float32)
        sums[0], sums[1] = lax.fori_loop(0, MOMENTS, add_channel, (zero, zero), unroll=4)
        even, odd = pl.ds(0, MOMENTS, stride=2), pl.ds(1, MOMENTS, stride=2)
        real_part = sums[0, even, :] - sums[1, odd, :]
        imag_part = sums[0, odd, :] + sums[1, even, :]
        real_roll, imag_roll = pltpu.roll(real_part, N, 1), pltpu.roll(imag_part, N, 1)
        for half in range(2):
            kz = 2 * pair + half
            if kz >= KEEP:
                continue
            low_real, high_real = (real_part, real_roll) if half == 0 else (real_roll, real_part)
            low_imag, high_imag = (imag_part, imag_roll) if half == 0 else (imag_roll, imag_part)
            coeff[pl.ds(kz, MOMENTS, stride=GROUP), :] = jnp.where(first_half, low_real, -high_imag)
            coeff[pl.ds(KEEP + kz, MOMENTS, stride=GROUP), :] = jnp.where(
                first_half, low_imag, high_real
            )
    high, low = split(coeff[...])
    scatter_lines(
        out, mxu_nt(inverse[...], jnp.concatenate([high, high, low], axis=1)), INVERSE
    )


def final_kernel(chunks, offsets, near, table, out, lines):
    lines[...] = jnp.zeros_like(lines)
    for channel in range(MOMENTS):
        for block in range(8):
            lines[8 * channel : 8 * channel + 8, block * GROUP : (block + 1) * GROUP] = chunks[
                block, :, channel * GROUP : (channel + 1) * GROUP
            ]
    high, low = split(lines[...])
    field = mxu(jnp.concatenate([high, low, high], axis=1), table[...])
    listed = channel_list()
    place = {powers_of: index for index, powers_of in enumerate(listed)}

    def coefficient(pow_x, pow_y, pow_z):
        index = place[(pow_x, pow_y, pow_z)]
        return field[8 * index : 8 * index + 8, :]

    for tile in range(4):
        where = slice(128 * tile, 128 * tile + 128)
        s = 2.0 * offsets[0, 0, :, where] - 1.0
        t = 2.0 * offsets[1, 0, :, where] - 1.0
        w = 2.0 * offsets[2, 0, :, where] - 1.0
        value, slope_s, slope_t = [], [], []
        for pow_z in range(2):
            inner, inner_slope = [], []
            for pow_x in range(6 - pow_z):
                top = 5 - pow_z - pow_x
                total = coefficient(pow_x, top, pow_z)
                slope = None
                for pow_y in range(top - 1, -1, -1):
                    slope = total if slope is None else slope * t + total
                    total = total * t + coefficient(pow_x, pow_y, pow_z)
                inner.append(total)
                inner_slope.append(slope)
            total, slope = inner[-1], None
            total_t = None
            for pow_x in range(len(inner) - 2, -1, -1):
                slope = total if slope is None else slope * s + total
                total = total * s + inner[pow_x]
                total_t = (
                    inner_slope[pow_x] if total_t is None else total_t * s + inner_slope[pow_x]
                )
            value.append(total)
            slope_s.append(slope)
            slope_t.append(total_t)
        out[0, 0, :, where] = near[0, :, where] - (slope_s[0] + w * slope_s[1])
        out[1, 0, :, where] = near[1, :, where] - (slope_t[0] + w * slope_t[1])
        out[2, 0, :, where] = near[2, :, where] - value[1]


def near_kernel(lines, own, out, planes):
    planes[1] = own[...]
    for row in range(3):
        for plane, lead in ((0, LEAD), (2, 2 * LEAD)):
            planes[plane, pl.ds(row, PIECES, stride=3), :] = lines[
                pl.ds(lead + row, PIECES, stride=INVERSE), :
            ]
    first_half = lax.broadcasted_iota(jnp.int32, (8, 128), 1) < N
    targets = [
        [own[pl.ds(TILE_ROWS * k + 4 + comp, 8, stride=4), :] for k in range(4)]
        for comp in range(3)
    ]

    def add_plane(plane, sums):
        sums = list(sums)
        for shift_y in (-1, 0, 1):
            for pair in range(4):
                window = [
                    planes[
                        plane,
                        pl.ds(TILE_ROWS * pair + 4 + 4 * shift_y + comp, 8, stride=4),
                        :,
                    ]
                    for comp in range(4)
                ]
                window[0] = window[0] + (plane - 1).astype(jnp.float32)
                window[1] = window[1] + float(shift_y)
                turned = [pltpu.roll(value, N, 1) for value in window]
                for half in range(2):
                    source = [
                        jnp.where(first_half, a, b) if half == 0 else jnp.where(first_half, b, a)
                        for a, b in zip(window, turned)
                    ]
                    for shift_z in (-1, 0, 1):
                        moved = source
                        if shift_z:
                            moved = [pltpu.roll(v, (128 - shift_z) % 128, 1) for v in source]
                            moved[2] = moved[2] + float(shift_z)
                        for k in range(4):
                            sep = [moved[comp] - targets[comp][k] for comp in range(3)]
                            squared = (sep[0] * sep[0] + sep[1] * sep[1]) + (
                                sep[2] * sep[2] + SOFTEN * SOFTEN
                            )
                            inverse = lax.rsqrt(squared)
                            weight = (moved[3] * inverse) * (inverse * inverse)
                            for comp in range(3):
                                sums[3 * k + comp] = sums[3 * k + comp] + sep[comp] * weight
        return tuple(sums)

    zero = jnp.zeros((8, 128), jnp.float32)
    sums = lax.fori_loop(0, 3, add_plane, (zero,) * 12)
    for k in range(4):
        for comp in range(3):
            out[comp, :, 128 * k : 128 * k + 128] = sums[3 * k + comp]


def shape(*dims, dtype=jnp.float32):
    return jax.ShapeDtypeStruct(dims, dtype)


def call(kernel, outs, scratch, cycles, in_specs=None, out_specs=None, aliases={}):
    block = pl.BlockSpec(memory_space=pltpu.VMEM)
    count = kernel.__code__.co_argcount - len(jax.tree.leaves(outs)) - len(scratch)
    return pl.pallas_call(
        kernel,
        out_shape=outs,
        in_specs=in_specs or [block] * count,
        out_specs=out_specs or jax.tree.map(lambda _: block, outs),
        input_output_aliases=aliases,
        scratch_shapes=scratch,
        compiler_params=pltpu.CompilerParams(vmem_limit_bytes=16 << 20),
        cost_estimate=pl.CostEstimate(flops=cycles * 1000, bytes_accessed=cycles, transcendentals=0),
    )


def far_memory(value):
    return pltpu.with_memory_space_constraint(jnp.asarray(value), pltpu.HBM)


def exchange_rows(value, axis):
    rows = value.reshape(N, 1, -1)
    rows = lax.all_to_all(rows, axis, split_axis=0, concat_axis=0, tiled=True)
    return rows.reshape(value.shape)


def stages(offsets, masses, kernel):
    hbm = pl.BlockSpec(memory_space=pltpu.HBM)
    table_z, table_y = table_z_forward(), table_left()
    gains = jnp.transpose(kernel[:, :, :, 0, :], (0, 2, 1, 3))
    chunks, packed, left, gains = call(
        moments_kernel,
        (
            shape(8, 8, LANES + EDGE),
            shape(4, 32, 128),
            shape(*table_y.shape, dtype=jnp.bfloat16),
            shape(MOMENTS, 2 * MOMENTS, LANES, dtype=jnp.bfloat16),
        ),
        [
            VMEM((3, 1, 8, 512), jnp.float32),
            VMEM((1, 8, 512), jnp.float32),
            VMEM(table_z.shape, jnp.bfloat16),
            VMEM((8 * MOMENTS, 128), jnp.float32),
            pltpu.SemaphoreType.DMA((4 + MOMENTS,)),
        ],
        2000,
        [hbm] * 5,
    )(*(far_memory(value) for value in (offsets, masses, table_z, table_y, gains)))
    chunks = lax.all_to_all(chunks, "gy", split_axis=0, concat_axis=0, tiled=True)
    lines, extended = call(
        y_forward_kernel, (shape(N * FORWARD, 128), shape(FLAT, 128)), [], 1000
    )(chunks, packed, left)
    lines = exchange_rows(lines, "gx")
    lines = call(
        spectrum_kernel,
        shape(N * INVERSE, 128),
        [
            VMEM((LANES, 128), jnp.float32),
            VMEM((2, 3, MOMENTS, 128), jnp.float32),
            VMEM((LANES, 128), jnp.float32),
            VMEM((2, 2 * MOMENTS, 128), jnp.float32),
        ],
        3000,
    )(lines, gains, jnp.asarray(table_x_forward()), jnp.asarray(table_x_inverse()))
    lines = exchange_rows(lines, "gx")
    near = call(near_kernel, shape(3, 8, 512), [VMEM((3, FLAT, 128), jnp.float32)], 6000)(
        lines, extended
    )
    lines = call(y_inverse_kernel, shape(N, LANES), [], 1000)(lines, left)
    chunks = lax.all_to_all(
        lines.reshape(8, 8, LANES), "gy", split_axis=0, concat_axis=0, tiled=True
    )
    return call(
        final_kernel, shape(3, 1, 8, 512), [VMEM((8 * MOMENTS, 128), jnp.float32)], 2000
    )(chunks, offsets, near, jnp.asarray(table_z_inverse()))


def solution(mesh):
    placed = (P(None, "gx", "gy", None), P("gx", "gy", None), P(None, None, None, "gx", "gy"))
    return jax.shard_map(
        stages, mesh=mesh, in_specs=placed, out_specs=P(None, "gx", "gy", None), check_vma=False
    )
```

```python
import math

import jax
import jax.numpy as jnp
import numpy as np
from jax import lax
from jax.experimental import pallas as pl
from jax.experimental.pallas import tpu as pltpu
from jax.sharding import PartitionSpec as P

SOFTEN = 0.5
N = 64
KEEP = 5
GROUP = 2 * KEEP
MOMENTS = 36
LANES = 384
VMEM = pltpu.VMEM


def channel_list():
    listed = []
    for pow_z in range(2):
        for pow_x in range(6 - pow_z):
            for pow_y in range(6 - pow_z - pow_x):
                listed.append((pow_x, pow_y, pow_z))
    return listed


def split_np(table):
    high = np.asarray(table, np.float32).astype(jnp.bfloat16)
    low = (np.asarray(table, np.float64) - high.astype(np.float64)).astype(jnp.bfloat16)
    return high, low


def angles(rows, columns):
    product = np.outer(np.asarray(rows), np.asarray(columns)) % N
    return product * (2.0 * math.pi / N)


def kept_kz():
    return np.array([8 * block + offset for block in range(8) for offset in range(KEEP)])


def table_z_forward():
    angle = angles(np.arange(N), kept_kz()).reshape(N, 8, 1, KEEP)
    both = np.concatenate([np.cos(angle), -np.sin(angle)], axis=2).reshape(N, 8 * GROUP)
    both = np.pad(both, ((0, 0), (0, 128 - 8 * GROUP)))
    high, low = split_np(both)
    return np.concatenate([high, low, high, np.zeros_like(high)], axis=0)


def table_left():
    angle = angles(np.arange(N), np.arange(N))
    high, low = split_np(np.concatenate([np.cos(angle), np.sin(angle)], axis=0))
    return np.concatenate([high, low, high], axis=1)


def table_x_forward():
    angle = angles(np.arange(N), np.arange(N))
    high, low = split_np(np.concatenate([np.cos(angle), np.sin(angle)], axis=1))
    return np.concatenate([high, low, high, np.zeros_like(high)], axis=0)


def table_x_inverse():
    angle = angles(np.arange(N), np.arange(N))
    high, low = split_np(np.concatenate([np.cos(angle), np.sin(angle)], axis=1))
    return np.concatenate([high, low, high], axis=1)


def table_z_inverse():
    angle = angles(kept_kz(), np.arange(N)).reshape(8, 1, KEEP, N)
    weight = np.where(np.arange(KEEP) % 4 == 0, 1.0, 2.0).reshape(1, 1, KEEP, 1)
    both = np.concatenate([np.cos(angle), -np.sin(angle)], axis=1) * weight / float(N**3)
    both = np.pad(both.reshape(8 * GROUP, N), ((0, 128 - 8 * GROUP), (0, 0)))
    both = np.concatenate([both, both], axis=1)
    high, low = split_np(both)
    return np.concatenate([high, high, low], axis=0)


def split(value):
    high = value.astype(jnp.bfloat16)
    low = (value - high.astype(jnp.float32)).astype(jnp.bfloat16)
    return high, low


def mxu(left, right):
    return jnp.dot(left, right, preferred_element_type=jnp.float32)


def mxu_nt(left, right):
    return lax.dot_general(
        left, right, (((1,), (1,)), ((), ())), preferred_element_type=jnp.float32
    )


def powers(values, highest):
    result = [None, values]
    for _ in range(highest - 1):
        result.append(result[-1] * values)
    return result


EDGE = 256
LEAD = 3
TILE_ROWS = 40
FLAT = 160
FORWARD, INVERSE = 6, 8


def edge_places(comp):
    for tile in range(4):
        index = 4 * comp + tile
        lane = LANES + 128 * (index % 2)
        yield tile, index // 2, slice(lane, lane + 128)


def moments_kernel(
    offsets_hbm,
    masses_hbm,
    table_hbm,
    left_hbm,
    gains_hbm,
    chunks,
    packed,
    left,
    gains,
    offsets,
    masses,
    table,
    moments,
    sems,
):
    pairs = (
        (offsets_hbm, offsets),
        (masses_hbm, masses),
        (table_hbm, table),
        (left_hbm, left),
    )
    pairs += tuple(
        (gains_hbm.at[row, :, :, pl.ds(0, LANES)], gains.at[:, pl.ds(2 * row, 2), :])
        for row in range(MOMENTS)
    )
    copies = [pltpu.make_async_copy(a, b, sems.at[i]) for i, (a, b) in enumerate(pairs)]
    for copy in copies:
        copy.start()
    me = lax.axis_index("gy")
    after, before = lax.rem(me + 1, 8), lax.rem(me + 7, 8)
    chunks[:, :, 256:] = jnp.zeros((8, 8, LANES + EDGE - 256), jnp.float32)
    copies[0].wait()
    copies[1].wait()
    mass = masses[0]
    for comp in range(4):
        value = offsets[comp, 0] if comp < 3 else mass
        for tile, row, lanes in edge_places(comp):
            part = value[:, 128 * tile : 128 * tile + 128]
            packed[tile, pl.ds(comp, 8, stride=4), :] = part
            chunks[after, row : row + 1, lanes] = part[7:8]
            chunks[before, row : row + 1, lanes] = part[0:1]
    along_x = powers(2.0 * offsets[0, 0] - 1.0, 5)
    along_y = powers(2.0 * offsets[1, 0] - 1.0, 5)
    along_z = 2.0 * offsets[2, 0] - 1.0
    channel = 0
    for pow_z in range(2):
        lead_z = mass * along_z if pow_z else mass
        for pow_x in range(6 - pow_z):
            lead = lead_z * along_x[pow_x] if pow_x else lead_z
            for pow_y in range(6 - pow_z - pow_x):
                term = lead * along_y[pow_y] if pow_y else lead
                part = (term[:, 0:128] + term[:, 128:256]) + (term[:, 256:384] + term[:, 384:512])
                moments[8 * channel : 8 * channel + 8, :] = part + pltpu.roll(part, 64, 1)
                channel += 1
    high, low = split(moments[...])
    copies[2].wait()
    lines = mxu(jnp.concatenate([high, low], axis=1), table[...])
    for channel in range(MOMENTS):
        rows = lines[8 * channel : 8 * channel + 8]
        for block in range(8):
            chunks[block, :, channel * GROUP : (channel + 1) * GROUP] = rows[
                :, block * GROUP : (block + 1) * GROUP
            ]
    for copy in copies[3:]:
        copy.wait()


def line_transform(lines, table, direction):
    high, low = split(lines)
    both = mxu(table, jnp.concatenate([high, high, low], axis=0))
    cos_part, sin_part = both[:N], both[N:]
    lane = lax.broadcasted_iota(jnp.int32, (1, LANES), 1)
    imag_lane = lax.rem(lane, GROUP) >= KEEP
    swapped = jnp.where(
        imag_lane, pltpu.roll(sin_part, KEEP, 1), pltpu.roll(sin_part, LANES - KEEP, 1)
    )
    factor = jnp.where(imag_lane, -1.0, 1.0) * direction
    return cos_part + swapped * factor


def gather_lines(lines, chunk):
    return jnp.concatenate([lines[pl.ds(row, N, stride=chunk), :] for row in range(LEAD)], axis=1)


def scatter_lines(out, result, chunk):
    for row in range(LEAD):
        out[pl.ds(row, N, stride=chunk), :] = result[:, 128 * row : 128 * row + 128]


def y_forward_kernel(chunks, packed, table, out, extended):
    me = lax.axis_index("gy")
    after, before = lax.rem(me + 1, 8), lax.rem(me + 7, 8)
    for tile in range(4):
        first = TILE_ROWS * tile
        extended[first + 4 : first + 36, :] = packed[tile]
    for comp in range(4):
        for tile, row, lanes in edge_places(comp):
            top = TILE_ROWS * tile + comp
            extended[top : top + 1, :] = chunks[before, row : row + 1, lanes]
            extended[top + 36 : top + 37, :] = chunks[after, row : row + 1, lanes]
    result = line_transform(chunks[:, :, :LANES].reshape(N, LANES), table[...], 1.0)
    scatter_lines(out, result, FORWARD)
    for row in range(2):
        out[pl.ds(LEAD + row, N, stride=FORWARD), :] = extended[pl.ds(row, N, stride=2), :]
    tail = extended[2 * N :, :]
    out[pl.ds(LEAD + 2, N // 2, stride=FORWARD), :] = tail
    out[pl.ds(FORWARD * N // 2 + LEAD + 2, N // 2, stride=FORWARD), :] = pltpu.roll(tail, N, 1)


def y_inverse_kernel(lines, table, out):
    out[...] = line_transform(gather_lines(lines, INVERSE), table[...], -1.0)


def spectrum_kernel(lines, gains, forward, inverse, out, rows, spec, coeff, sums):
    half = lax.broadcasted_iota(jnp.int32, (1, 128), 1) < N

    def relay(row, start, count, prior, following):
        ahead = lines[pl.ds(FORWARD * prior + row, count, stride=FORWARD), :]
        behind = lines[pl.ds(FORWARD * following + row, count, stride=FORWARD), :]
        first = INVERSE * start + 2 * row - LEAD
        rows = pl.ds(first, count, stride=INVERSE)
        out[rows, :] = jnp.where(half, ahead, pltpu.roll(behind, N, 1))
        if row < 2 * LEAD - 1:
            rows = pl.ds(first + 1, count, stride=INVERSE)
            out[rows, :] = jnp.where(half, pltpu.roll(ahead, N, 1), behind)

    for row in range(LEAD, 2 * LEAD):
        relay(row, 1, N - 2, 0, 2)
        relay(row, 0, 1, N - 1, 1)
        relay(row, N - 1, 1, N - 2, 0)
    gathered = gather_lines(lines, FORWARD)
    turned = jnp.concatenate([gathered, gathered], axis=0).T
    high, low = split(turned)
    rows[...] = mxu(jnp.concatenate([high, low], axis=1), forward[...])
    first_half = lax.broadcasted_iota(jnp.int32, (1, 128), 1) < N
    real_first, imag_first = [], []
    for kz in range(KEEP):
        real_part = rows[pl.ds(kz, MOMENTS, stride=GROUP), :]
        imag_part = rows[pl.ds(KEEP + kz, MOMENTS, stride=GROUP), :]
        both = jnp.where(first_half, real_part, -real_part) + pltpu.roll(imag_part, N, 1)
        real_first.append(both)
        imag_first.append(pltpu.roll(both, N, 1))
    real_first.append(real_first[-1])
    imag_first.append(imag_first[-1])
    for pair in range(3):
        spec[0, pair] = jnp.where(first_half, real_first[2 * pair], imag_first[2 * pair + 1])
        spec[1, pair] = jnp.where(first_half, imag_first[2 * pair], real_first[2 * pair + 1])

    coeff[...] = jnp.zeros_like(coeff)
    for pair in range(3):
        where = slice(128 * pair, 128 * pair + 128)

        def add_channel(channel, running):
            by_real, by_imag = running
            gain = gains[channel, :, where].astype(jnp.float32)
            by_real = by_real + gain * spec[0, pair, pl.ds(channel, 1), :]
            by_imag = by_imag + gain * spec[1, pair, pl.ds(channel, 1), :]
            return by_real, by_imag

        zero = jnp.zeros((2 * MOMENTS, 128), jnp.float32)
        sums[0], sums[1] = lax.fori_loop(0, MOMENTS, add_channel, (zero, zero), unroll=4)
        even, odd = pl.ds(0, MOMENTS, stride=2), pl.ds(1, MOMENTS, stride=2)
        real_part = sums[0, even, :] - sums[1, odd, :]
        imag_part = sums[0, odd, :] + sums[1, even, :]
        real_roll, imag_roll = pltpu.roll(real_part, N, 1), pltpu.roll(imag_part, N, 1)
        for half in range(2):
            kz = 2 * pair + half
            if kz >= KEEP:
                continue
            low_real, high_real = (real_part, real_roll) if half == 0 else (real_roll, real_part)
            low_imag, high_imag = (imag_part, imag_roll) if half == 0 else (imag_roll, imag_part)
            coeff[pl.ds(kz, MOMENTS, stride=GROUP), :] = jnp.where(first_half, low_real, -high_imag)
            coeff[pl.ds(KEEP + kz, MOMENTS, stride=GROUP), :] = jnp.where(
                first_half, low_imag, high_real
            )
    high, low = split(coeff[...])
    scatter_lines(
        out, mxu_nt(inverse[...], jnp.concatenate([high, high, low], axis=1)), INVERSE
    )


def final_kernel(chunks, offsets, near, table, out, lines):
    lines[...] = jnp.zeros_like(lines)
    for channel in range(MOMENTS):
        for block in range(8):
            lines[8 * channel : 8 * channel + 8, block * GROUP : (block + 1) * GROUP] = chunks[
                block, :, channel * GROUP : (channel + 1) * GROUP
            ]
    high, low = split(lines[...])
    field = mxu(jnp.concatenate([high, low, high], axis=1), table[...])
    listed = channel_list()
    place = {powers_of: index for index, powers_of in enumerate(listed)}

    def coefficient(pow_x, pow_y, pow_z):
        index = place[(pow_x, pow_y, pow_z)]
        return field[8 * index : 8 * index + 8, :]

    for tile in range(4):
        where = slice(128 * tile, 128 * tile + 128)
        s = 2.0 * offsets[0, 0, :, where] - 1.0
        t = 2.0 * offsets[1, 0, :, where] - 1.0
        w = 2.0 * offsets[2, 0, :, where] - 1.0
        value, slope_s, slope_t = [], [], []
        for pow_z in range(2):
            inner, inner_slope = [], []
            for pow_x in range(6 - pow_z):
                top = 5 - pow_z - pow_x
                total = coefficient(pow_x, top, pow_z)
                slope = None
                for pow_y in range(top - 1, -1, -1):
                    slope = total if slope is None else slope * t + total
                    total = total * t + coefficient(pow_x, pow_y, pow_z)
                inner.append(total)
                inner_slope.append(slope)
            total, slope = inner[-1], None
            total_t = None
            for pow_x in range(len(inner) - 2, -1, -1):
                slope = total if slope is None else slope * s + total
                total = total * s + inner[pow_x]
                total_t = (
                    inner_slope[pow_x] if total_t is None else total_t * s + inner_slope[pow_x]
                )
            value.append(total)
            slope_s.append(slope)
            slope_t.append(total_t)
        out[0, 0, :, where] = near[0, :, where] - (slope_s[0] + w * slope_s[1])
        out[1, 0, :, where] = near[1, :, where] - (slope_t[0] + w * slope_t[1])
        out[2, 0, :, where] = near[2, :, where] - value[1]


def near_kernel(lines, own, out, planes):
    planes[1] = own[...]
    half = lax.broadcasted_iota(jnp.int32, (1, 128), 1) < N

    def unpack(rows, low, high):
        planes[0, rows, :] = jnp.where(half, low, pltpu.roll(high, N, 1))
        planes[2, rows, :] = jnp.where(half, pltpu.roll(low, N, 1), high)

    for row in range(2):
        low, high = (
            lines[pl.ds(LEAD + 2 * row + side, N, stride=INVERSE), :] for side in range(2)
        )
        unpack(pl.ds(row, N, stride=2), low, high)
    low, high = (
        lines[pl.ds(INVERSE * N // 2 * side + INVERSE - 1, N // 2, stride=INVERSE), :]
        for side in range(2)
    )
    unpack(pl.ds(2 * N, N // 2), low, high)
    first_half = lax.broadcasted_iota(jnp.int32, (8, 128), 1) < N
    targets = [
        [own[pl.ds(TILE_ROWS * k + 4 + comp, 8, stride=4), :] for k in range(4)]
        for comp in range(3)
    ]

    def add_plane(plane, sums):
        sums = list(sums)
        for shift_y in (-1, 0, 1):
            for pair in range(4):
                window = [
                    planes[
                        plane,
                        pl.ds(TILE_ROWS * pair + 4 + 4 * shift_y + comp, 8, stride=4),
                        :,
                    ]
                    for comp in range(4)
                ]
                window[0] = window[0] + (plane - 1).astype(jnp.float32)
                window[1] = window[1] + float(shift_y)
                turned = [pltpu.roll(value, N, 1) for value in window]
                for half in range(2):
                    source = [
                        jnp.where(first_half, a, b) if half == 0 else jnp.where(first_half, b, a)
                        for a, b in zip(window, turned)
                    ]
                    for shift_z in (-1, 0, 1):
                        moved = source
                        if shift_z:
                            moved = [pltpu.roll(v, (128 - shift_z) % 128, 1) for v in source]
                            moved[2] = moved[2] + float(shift_z)
                        for k in range(4):
                            sep = [moved[comp] - targets[comp][k] for comp in range(3)]
                            squared = (sep[0] * sep[0] + sep[1] * sep[1]) + (
                                sep[2] * sep[2] + SOFTEN * SOFTEN
                            )
                            inverse = lax.rsqrt(squared)
                            weight = (moved[3] * inverse) * (inverse * inverse)
                            for comp in range(3):
                                sums[3 * k + comp] = sums[3 * k + comp] + sep[comp] * weight
        return tuple(sums)

    zero = jnp.zeros((8, 128), jnp.float32)
    sums = lax.fori_loop(0, 3, add_plane, (zero,) * 12)
    for k in range(4):
        for comp in range(3):
            out[comp, :, 128 * k : 128 * k + 128] = sums[3 * k + comp]


def shape(*dims, dtype=jnp.float32):
    return jax.ShapeDtypeStruct(dims, dtype)


def call(kernel, outs, scratch, cycles, in_specs=None, out_specs=None, aliases={}):
    block = pl.BlockSpec(memory_space=pltpu.VMEM)
    count = kernel.__code__.co_argcount - len(jax.tree.leaves(outs)) - len(scratch)
    return pl.pallas_call(
        kernel,
        out_shape=outs,
        in_specs=in_specs or [block] * count,
        out_specs=out_specs or jax.tree.map(lambda _: block, outs),
        input_output_aliases=aliases,
        scratch_shapes=scratch,
        compiler_params=pltpu.CompilerParams(vmem_limit_bytes=16 << 20),
        cost_estimate=pl.CostEstimate(flops=cycles * 1000, bytes_accessed=cycles, transcendentals=0),
    )


def far_memory(value):
    return pltpu.with_memory_space_constraint(jnp.asarray(value), pltpu.HBM)


def exchange_rows(value, axis):
    rows = value.reshape((N, 8, 128) if value.shape[0] == 8 * N else (N, 1, -1))
    rows = lax.all_to_all(rows, axis, split_axis=0, concat_axis=0, tiled=True)
    return rows.reshape(value.shape)


def stages(offsets, masses, kernel):
    hbm = pl.BlockSpec(memory_space=pltpu.HBM)
    table_z, table_y = table_z_forward(), table_left()
    matrices = jnp.transpose(kernel[:, :, :, 0, :], (0, 2, 1, 3))
    chunks, packed, left, gains = call(
        moments_kernel,
        (
            shape(8, 8, LANES + EDGE),
            shape(4, 32, 128),
            shape(*table_y.shape, dtype=jnp.bfloat16),
            shape(MOMENTS, 2 * MOMENTS, LANES, dtype=jnp.bfloat16),
        ),
        [
            VMEM((3, 1, 8, 512), jnp.float32),
            VMEM((1, 8, 512), jnp.float32),
            VMEM(table_z.shape, jnp.bfloat16),
            VMEM((8 * MOMENTS, 128), jnp.float32),
            pltpu.SemaphoreType.DMA((4 + MOMENTS,)),
        ],
        2000,
        [hbm] * 5,
    )(*(far_memory(value) for value in (offsets, masses, table_z, table_y, matrices)))
    chunks = lax.all_to_all(chunks, "gy", split_axis=0, concat_axis=0, tiled=True)
    lines, extended = call(
        y_forward_kernel, (shape(N * FORWARD, 128), shape(FLAT, 128)), [], 1000
    )(chunks, packed, left)
    lines = exchange_rows(lines, "gx")
    lines = call(
        spectrum_kernel,
        shape(N * INVERSE, 128),
        [
            VMEM((LANES, 128), jnp.float32),
            VMEM((2, 3, MOMENTS, 128), jnp.float32),
            VMEM((LANES, 128), jnp.float32),
            VMEM((2, 2 * MOMENTS, 128), jnp.float32),
        ],
        3000,
    )(lines, gains, jnp.asarray(table_x_forward()), jnp.asarray(table_x_inverse()))
    lines = exchange_rows(lines, "gx")
    near = call(near_kernel, shape(3, 8, 512), [VMEM((3, FLAT, 128), jnp.float32)], 6000)(
        lines, extended
    )
    lines = call(y_inverse_kernel, shape(N, LANES), [], 1000)(lines, left)
    chunks = lax.all_to_all(
        lines.reshape(8, 8, LANES), "gy", split_axis=0, concat_axis=0, tiled=True
    )
    return call(
        final_kernel, shape(3, 1, 8, 512), [VMEM((8 * MOMENTS, 128), jnp.float32)], 2000
    )(chunks, offsets, near, jnp.asarray(table_z_inverse()))


def solution(mesh):
    placed = (P(None, "gx", "gy", None), P("gx", "gy", None), P(None, None, None, "gx", "gy"))
    return jax.shard_map(
        stages, mesh=mesh, in_specs=placed, out_specs=P(None, "gx", "gy", None), check_vma=False
    )
```

```python
import math

import jax
import jax.numpy as jnp
import numpy as np
from jax import lax
from jax.experimental import pallas as pl
from jax.experimental.pallas import tpu as pltpu
from jax.sharding import PartitionSpec as P

SOFTEN = 0.5
N = 64
KEEP = 5
GROUP = 2 * KEEP
MOMENTS = 36
LANES = 384
VMEM = pltpu.VMEM


def channel_list():
    listed = []
    for pow_z in range(2):
        for pow_x in range(6 - pow_z):
            for pow_y in range(6 - pow_z - pow_x):
                listed.append((pow_x, pow_y, pow_z))
    return listed


def split_np(table):
    high = np.asarray(table, np.float32).astype(jnp.bfloat16)
    low = (np.asarray(table, np.float64) - high.astype(np.float64)).astype(jnp.bfloat16)
    return high, low


def angles(rows, columns):
    product = np.outer(np.asarray(rows), np.asarray(columns)) % N
    return product * (2.0 * math.pi / N)


def kept_kz():
    return np.array([8 * block + offset for block in range(8) for offset in range(KEEP)])


def table_z_forward():
    angle = angles(np.arange(N), kept_kz()).reshape(N, 8, 1, KEEP)
    both = np.concatenate([np.cos(angle), -np.sin(angle)], axis=2).reshape(N, 8 * GROUP)
    both = np.pad(both, ((0, 0), (0, 128 - 8 * GROUP)))
    high, low = split_np(both)
    return np.concatenate([high, low, high, np.zeros_like(high)], axis=0)


def table_left():
    angle = angles(np.arange(N), np.arange(N))
    high, low = split_np(np.concatenate([np.cos(angle), np.sin(angle)], axis=0))
    return np.concatenate([high, low, high], axis=1)


def table_x_forward():
    angle = angles(np.arange(N), np.arange(N))
    high, low = split_np(np.concatenate([np.cos(angle), np.sin(angle)], axis=1))
    return np.concatenate([high, low, high, np.zeros_like(high)], axis=0)


def table_x_inverse():
    angle = angles(np.arange(N), np.arange(N))
    high, low = split_np(np.concatenate([np.cos(angle), np.sin(angle)], axis=1))
    return np.concatenate([high, low, high], axis=1)


def table_z_inverse():
    angle = angles(kept_kz(), np.arange(N)).reshape(8, 1, KEEP, N)
    weight = np.where(np.arange(KEEP) % 4 == 0, 1.0, 2.0).reshape(1, 1, KEEP, 1)
    both = np.concatenate([np.cos(angle), -np.sin(angle)], axis=1) * weight / float(N**3)
    both = np.pad(both.reshape(8 * GROUP, N), ((0, 128 - 8 * GROUP), (0, 0)))
    both = np.concatenate([both, both], axis=1)
    high, low = split_np(both)
    return np.concatenate([high, high, low], axis=0)


def split(value):
    high = value.astype(jnp.bfloat16)
    low = (value - high.astype(jnp.float32)).astype(jnp.bfloat16)
    return high, low


def mxu(left, right):
    return jnp.dot(left, right, preferred_element_type=jnp.float32)


def mxu_nt(left, right):
    return lax.dot_general(
        left, right, (((1,), (1,)), ((), ())), preferred_element_type=jnp.float32
    )


def powers(values, highest):
    result = [None, values]
    for _ in range(highest - 1):
        result.append(result[-1] * values)
    return result


EDGE = 256
LEAD = 3
TILE_ROWS = 40
FLAT = 160
FORWARD, INVERSE = 6, 8


def edge_places(comp):
    for tile in range(4):
        index = 4 * comp + tile
        lane = LANES + 128 * (index % 2)
        yield tile, index // 2, slice(lane, lane + 128)


def moments_kernel(
    offsets_hbm,
    masses_hbm,
    table_hbm,
    left_hbm,
    gains_hbm,
    chunks,
    packed,
    left,
    gains,
    offsets,
    masses,
    table,
    moments,
    sems,
):
    pairs = (
        (offsets_hbm, offsets),
        (masses_hbm, masses),
        (table_hbm, table),
        (left_hbm, left),
    )
    pairs += tuple(
        (gains_hbm.at[row, :, :, pl.ds(0, LANES)], gains.at[:, pl.ds(2 * row, 2), :])
        for row in range(MOMENTS)
    )
    copies = [pltpu.make_async_copy(a, b, sems.at[i]) for i, (a, b) in enumerate(pairs)]
    for copy in copies:
        copy.start()
    me = lax.axis_index("gy")
    after, before = lax.rem(me + 1, 8), lax.rem(me + 7, 8)
    chunks[:, :, 256:] = jnp.zeros((8, 8, LANES + EDGE - 256), jnp.float32)
    copies[0].wait()
    copies[1].wait()
    mass = masses[0]
    for comp in range(4):
        value = offsets[comp, 0] if comp < 3 else mass
        for tile, row, lanes in edge_places(comp):
            part = value[:, 128 * tile : 128 * tile + 128]
            packed[tile, pl.ds(comp, 8, stride=4), :] = part
            chunks[after, row : row + 1, lanes] = part[7:8]
            chunks[before, row : row + 1, lanes] = part[0:1]
    along_x = powers(2.0 * offsets[0, 0] - 1.0, 5)
    along_y = powers(2.0 * offsets[1, 0] - 1.0, 5)
    along_z = 2.0 * offsets[2, 0] - 1.0
    channel = 0
    for pow_z in range(2):
        lead_z = mass * along_z if pow_z else mass
        for pow_x in range(6 - pow_z):
            lead = lead_z * along_x[pow_x] if pow_x else lead_z
            for pow_y in range(6 - pow_z - pow_x):
                term = lead * along_y[pow_y] if pow_y else lead
                part = (term[:, 0:128] + term[:, 128:256]) + (term[:, 256:384] + term[:, 384:512])
                moments[8 * channel : 8 * channel + 8, :] = part + pltpu.roll(part, 64, 1)
                channel += 1
    high, low = split(moments[...])
    copies[2].wait()
    lines = mxu(jnp.concatenate([high, low], axis=1), table[...])
    for channel in range(MOMENTS):
        rows = lines[8 * channel : 8 * channel + 8]
        for block in range(8):
            chunks[block, :, channel * GROUP : (channel + 1) * GROUP] = rows[
                :, block * GROUP : (block + 1) * GROUP
            ]
    for copy in copies[3:]:
        copy.wait()


def line_transform(lines, table, direction):
    high, low = split(lines)
    both = mxu(table, jnp.concatenate([high, high, low], axis=0))
    cos_part, sin_part = both[:N], both[N:]
    lane = lax.broadcasted_iota(jnp.int32, (1, LANES), 1)
    imag_lane = lax.rem(lane, GROUP) >= KEEP
    swapped = jnp.where(
        imag_lane, pltpu.roll(sin_part, KEEP, 1), pltpu.roll(sin_part, LANES - KEEP, 1)
    )
    factor = jnp.where(imag_lane, -1.0, 1.0) * direction
    return cos_part + swapped * factor


def gather_lines(lines, chunk):
    return jnp.concatenate([lines[pl.ds(row, N, stride=chunk), :] for row in range(LEAD)], axis=1)


def scatter_lines(out, result, chunk):
    for row in range(LEAD):
        out[pl.ds(row, N, stride=chunk), :] = result[:, 128 * row : 128 * row + 128]


def y_forward_kernel(chunks, packed, table, out, extended):
    me = lax.axis_index("gy")
    after, before = lax.rem(me + 1, 8), lax.rem(me + 7, 8)
    for tile in range(4):
        first = TILE_ROWS * tile
        extended[first + 4 : first + 36, :] = packed[tile]
    for comp in range(4):
        for tile, row, lanes in edge_places(comp):
            top = TILE_ROWS * tile + comp
            extended[top : top + 1, :] = chunks[before, row : row + 1, lanes]
            extended[top + 36 : top + 37, :] = chunks[after, row : row + 1, lanes]
    result = line_transform(chunks[:, :, :LANES].reshape(N, LANES), table[...], 1.0)
    scatter_lines(out, result, FORWARD)
    for row in range(2):
        out[pl.ds(LEAD + row, N, stride=FORWARD), :] = extended[pl.ds(row, N, stride=2), :]
    tail = extended[2 * N :, :]
    out[pl.ds(LEAD + 2, N // 2, stride=FORWARD), :] = tail
    out[pl.ds(FORWARD * N // 2 + LEAD + 2, N // 2, stride=FORWARD), :] = pltpu.roll(tail, N, 1)


def y_inverse_kernel(lines, table, out):
    out[...] = line_transform(gather_lines(lines, INVERSE), table[...], -1.0)


def spectrum_kernel(lines, gains, forward, inverse, out, rows, spec, coeff, sums):
    half = lax.broadcasted_iota(jnp.int32, (1, 128), 1) < N

    def relay(row, start, count, prior, following):
        ahead = lines[pl.ds(FORWARD * prior + row, count, stride=FORWARD), :]
        behind = lines[pl.ds(FORWARD * following + row, count, stride=FORWARD), :]
        first = INVERSE * start + 2 * row - LEAD
        rows = pl.ds(first, count, stride=INVERSE)
        out[rows, :] = jnp.where(half, ahead, pltpu.roll(behind, N, 1))
        if row < 2 * LEAD - 1:
            rows = pl.ds(first + 1, count, stride=INVERSE)
            out[rows, :] = jnp.where(half, pltpu.roll(ahead, N, 1), behind)

    for row in range(LEAD, 2 * LEAD):
        relay(row, 1, N - 2, 0, 2)
        relay(row, 0, 1, N - 1, 1)
        relay(row, N - 1, 1, N - 2, 0)
    gathered = gather_lines(lines, FORWARD)
    turned = jnp.concatenate([gathered, gathered], axis=0).T
    high, low = split(turned)
    rows[...] = mxu(jnp.concatenate([high, low], axis=1), forward[...])
    first_half = lax.broadcasted_iota(jnp.int32, (1, 128), 1) < N
    real_first, imag_first = [], []
    for kz in range(KEEP):
        real_part = rows[pl.ds(kz, MOMENTS, stride=GROUP), :]
        imag_part = rows[pl.ds(KEEP + kz, MOMENTS, stride=GROUP), :]
        both = jnp.where(first_half, real_part, -real_part) + pltpu.roll(imag_part, N, 1)
        real_first.append(both)
        imag_first.append(pltpu.roll(both, N, 1))
    real_first.append(real_first[-1])
    imag_first.append(imag_first[-1])
    for pair in range(3):
        spec[0, pair] = jnp.where(first_half, real_first[2 * pair], imag_first[2 * pair + 1])
        spec[1, pair] = jnp.where(first_half, imag_first[2 * pair], real_first[2 * pair + 1])

    used = MOMENTS * GROUP
    coeff[used:, :] = jnp.zeros((LANES - used, 128), jnp.float32)
    for pair in range(3):
        where = slice(128 * pair, 128 * pair + 128)

        def add_channel(channel, running):
            by_real, by_imag = running
            gain = gains[channel, :, where].astype(jnp.float32)
            by_real = by_real + gain * spec[0, pair, pl.ds(channel, 1), :]
            by_imag = by_imag + gain * spec[1, pair, pl.ds(channel, 1), :]
            return by_real, by_imag

        zero = jnp.zeros((2 * MOMENTS, 128), jnp.float32)
        sums[0], sums[1] = lax.fori_loop(0, MOMENTS, add_channel, (zero, zero), unroll=MOMENTS)
        even, odd = pl.ds(0, MOMENTS, stride=2), pl.ds(1, MOMENTS, stride=2)
        real_part = sums[0, even, :] - sums[1, odd, :]
        imag_part = sums[0, odd, :] + sums[1, even, :]
        real_roll, imag_roll = pltpu.roll(real_part, N, 1), pltpu.roll(imag_part, N, 1)
        for half in range(2):
            kz = 2 * pair + half
            if kz >= KEEP:
                continue
            low_real, high_real = (real_part, real_roll) if half == 0 else (real_roll, real_part)
            low_imag, high_imag = (imag_part, imag_roll) if half == 0 else (imag_roll, imag_part)
            coeff[pl.ds(kz, MOMENTS, stride=GROUP), :] = jnp.where(first_half, low_real, -high_imag)
            coeff[pl.ds(KEEP + kz, MOMENTS, stride=GROUP), :] = jnp.where(
                first_half, low_imag, high_real
            )
    high, low = split(coeff[...])
    scatter_lines(
        out, mxu_nt(inverse[...], jnp.concatenate([high, high, low], axis=1)), INVERSE
    )


def final_kernel(chunks, offsets, near, table, out, lines):
    lines[...] = jnp.zeros_like(lines)
    for channel in range(MOMENTS):
        for block in range(8):
            lines[8 * channel : 8 * channel + 8, block * GROUP : (block + 1) * GROUP] = chunks[
                block, :, channel * GROUP : (channel + 1) * GROUP
            ]
    high, low = split(lines[...])
    field = mxu(jnp.concatenate([high, low, high], axis=1), table[...])
    listed = channel_list()
    place = {powers_of: index for index, powers_of in enumerate(listed)}

    def coefficient(pow_x, pow_y, pow_z):
        index = place[(pow_x, pow_y, pow_z)]
        return field[8 * index : 8 * index + 8, :]

    for tile in range(4):
        where = slice(128 * tile, 128 * tile + 128)
        s = 2.0 * offsets[0, 0, :, where] - 1.0
        t = 2.0 * offsets[1, 0, :, where] - 1.0
        w = 2.0 * offsets[2, 0, :, where] - 1.0
        value, slope_s, slope_t = [], [], []
        for pow_z in range(2):
            inner, inner_slope = [], []
            for pow_x in range(6 - pow_z):
                top = 5 - pow_z - pow_x
                total = coefficient(pow_x, top, pow_z)
                slope = None
                for pow_y in range(top - 1, -1, -1):
                    slope = total if slope is None else slope * t + total
                    total = total * t + coefficient(pow_x, pow_y, pow_z)
                inner.append(total)
                inner_slope.append(slope)
            total, slope = inner[-1], None
            total_t = None
            for pow_x in range(len(inner) - 2, -1, -1):
                slope = total if slope is None else slope * s + total
                total = total * s + inner[pow_x]
                total_t = (
                    inner_slope[pow_x] if total_t is None else total_t * s + inner_slope[pow_x]
                )
            value.append(total)
            slope_s.append(slope)
            slope_t.append(total_t)
        out[0, 0, :, where] = near[0, :, where] - (slope_s[0] + w * slope_s[1])
        out[1, 0, :, where] = near[1, :, where] - (slope_t[0] + w * slope_t[1])
        out[2, 0, :, where] = near[2, :, where] - value[1]


def near_kernel(lines, own, out, planes):
    planes[1] = own[...]
    half = lax.broadcasted_iota(jnp.int32, (1, 128), 1) < N

    def unpack(rows, low, high):
        planes[0, rows, :] = jnp.where(half, low, pltpu.roll(high, N, 1))
        planes[2, rows, :] = jnp.where(half, pltpu.roll(low, N, 1), high)

    for row in range(2):
        low, high = (
            lines[pl.ds(LEAD + 2 * row + side, N, stride=INVERSE), :] for side in range(2)
        )
        unpack(pl.ds(row, N, stride=2), low, high)
    low, high = (
        lines[pl.ds(INVERSE * N // 2 * side + INVERSE - 1, N // 2, stride=INVERSE), :]
        for side in range(2)
    )
    unpack(pl.ds(2 * N, N // 2), low, high)
    first_half = lax.broadcasted_iota(jnp.int32, (8, 128), 1) < N
    targets = [
        [own[pl.ds(TILE_ROWS * k + 4 + comp, 8, stride=4), :] for k in range(4)]
        for comp in range(3)
    ]

    def add_plane(plane, sums):
        sums = list(sums)
        for shift_y in (-1, 0, 1):
            for pair in range(4):
                window = [
                    planes[
                        plane,
                        pl.ds(TILE_ROWS * pair + 4 + 4 * shift_y + comp, 8, stride=4),
                        :,
                    ]
                    for comp in range(4)
                ]
                window[0] = window[0] + (plane - 1).astype(jnp.float32)
                window[1] = window[1] + float(shift_y)
                turned = [pltpu.roll(value, N, 1) for value in window]
                for half in range(2):
                    source = [
                        jnp.where(first_half, a, b) if half == 0 else jnp.where(first_half, b, a)
                        for a, b in zip(window, turned)
                    ]
                    for shift_z in (-1, 0, 1):
                        moved = source
                        if shift_z:
                            moved = [pltpu.roll(v, (128 - shift_z) % 128, 1) for v in source]
                            moved[2] = moved[2] + float(shift_z)
                        for k in range(4):
                            sep = [moved[comp] - targets[comp][k] for comp in range(3)]
                            squared = (sep[0] * sep[0] + sep[1] * sep[1]) + (
                                sep[2] * sep[2] + SOFTEN * SOFTEN
                            )
                            inverse = lax.rsqrt(squared)
                            weight = (moved[3] * inverse) * (inverse * inverse)
                            for comp in range(3):
                                sums[3 * k + comp] = sums[3 * k + comp] + sep[comp] * weight
        return tuple(sums)

    zero = jnp.zeros((8, 128), jnp.float32)
    sums = lax.fori_loop(0, 3, add_plane, (zero,) * 12)
    for k in range(4):
        for comp in range(3):
            out[comp, :, 128 * k : 128 * k + 128] = sums[3 * k + comp]


def shape(*dims, dtype=jnp.float32):
    return jax.ShapeDtypeStruct(dims, dtype)


def call(kernel, outs, scratch, cycles, in_specs=None, out_specs=None, aliases={}):
    block = pl.BlockSpec(memory_space=pltpu.VMEM)
    count = kernel.__code__.co_argcount - len(jax.tree.leaves(outs)) - len(scratch)
    return pl.pallas_call(
        kernel,
        out_shape=outs,
        in_specs=in_specs or [block] * count,
        out_specs=out_specs or jax.tree.map(lambda _: block, outs),
        input_output_aliases=aliases,
        scratch_shapes=scratch,
        compiler_params=pltpu.CompilerParams(vmem_limit_bytes=16 << 20),
        cost_estimate=pl.CostEstimate(flops=cycles * 1000, bytes_accessed=cycles, transcendentals=0),
    )


def far_memory(value):
    return pltpu.with_memory_space_constraint(jnp.asarray(value), pltpu.HBM)


def exchange_rows(value, axis):
    rows = value.reshape((N, 8, 128) if value.shape[0] == 8 * N else (N, 1, -1))
    rows = lax.all_to_all(rows, axis, split_axis=0, concat_axis=0, tiled=True)
    return rows.reshape(value.shape)


def stages(offsets, masses, kernel):
    hbm = pl.BlockSpec(memory_space=pltpu.HBM)
    table_z, table_y = table_z_forward(), table_left()
    matrices = jnp.transpose(kernel[:, :, :, 0, :], (0, 2, 1, 3))
    chunks, packed, left, gains = call(
        moments_kernel,
        (
            shape(8, 8, LANES + EDGE),
            shape(4, 32, 128),
            shape(*table_y.shape, dtype=jnp.bfloat16),
            shape(MOMENTS, 2 * MOMENTS, LANES, dtype=jnp.bfloat16),
        ),
        [
            VMEM((3, 1, 8, 512), jnp.float32),
            VMEM((1, 8, 512), jnp.float32),
            VMEM(table_z.shape, jnp.bfloat16),
            VMEM((8 * MOMENTS, 128), jnp.float32),
            pltpu.SemaphoreType.DMA((4 + MOMENTS,)),
        ],
        2000,
        [hbm] * 5,
    )(*(far_memory(value) for value in (offsets, masses, table_z, table_y, matrices)))
    chunks = lax.all_to_all(chunks, "gy", split_axis=0, concat_axis=0, tiled=True)
    lines, extended = call(
        y_forward_kernel, (shape(N * FORWARD, 128), shape(FLAT, 128)), [], 1000
    )(chunks, packed, left)
    lines = exchange_rows(lines, "gx")
    lines = call(
        spectrum_kernel,
        shape(N * INVERSE, 128),
        [
            VMEM((LANES, 128), jnp.float32),
            VMEM((2, 3, MOMENTS, 128), jnp.float32),
            VMEM((LANES, 128), jnp.float32),
            VMEM((2, 2 * MOMENTS, 128), jnp.float32),
        ],
        3000,
    )(lines, gains, jnp.asarray(table_x_forward()), jnp.asarray(table_x_inverse()))
    lines = exchange_rows(lines, "gx")
    near = call(near_kernel, shape(3, 8, 512), [VMEM((3, FLAT, 128), jnp.float32)], 6000)(
        lines, extended
    )
    lines = call(y_inverse_kernel, shape(N, LANES), [], 1000)(lines, left)
    chunks = lax.all_to_all(
        lines.reshape(8, 8, LANES), "gy", split_axis=0, concat_axis=0, tiled=True
    )
    return call(
        final_kernel, shape(3, 1, 8, 512), [VMEM((8 * MOMENTS, 128), jnp.float32)], 2000
    )(chunks, offsets, near, jnp.asarray(table_z_inverse()))


def solution(mesh):
    placed = (P(None, "gx", "gy", None), P("gx", "gy", None), P(None, None, None, "gx", "gy"))
    return jax.shard_map(
        stages, mesh=mesh, in_specs=placed, out_specs=P(None, "gx", "gy", None), check_vma=False
    )
```
